512 devices in a mesh: rows: 64 (over y, x, core), dates: 8 (over z).
Axes of the slice: x: 4, y: 8, z: 8, core: 2. Of those that a mesh axis runs over, the one named last changes fastest.
Arguments:
- obs_mask: int32 [16, 512, 4096], P('dates', 'rows'), may hold values 0 or 1
- precision: float32 [16, 512, 4096], P('dates', 'rows'), may hold values from 0.5 to 4
- observed: float32 [16, 512, 4096], P('dates', 'rows')
- edge_class: int32 [2, 512, 4096], P(None, 'rows'), may hold values from 0 to 7
- temporal_weight: float32 [15], replicated, may hold values from 0.5 to 4
- inverse: bfloat16 [16, 16, 512, 4096], P(None, None, 'rows', 'dates'), as said below
Outputs:
- solution: float32 [16, 512, 4096], P('dates', 'rows')
- residual: float32 [16, 512, 4096], P('dates', 'rows')
The draws below stay inside these ranges and needn't reach their ends.
Inputs may be any that keep to these rules, and one draw needn't show every extreme that they name: `inverse`: each pixel's matrix is symmetric with a diagonal larger than the sum of magnitudes of its row's other entries.
All inputs are finite; a program needn't handle non-finite values. No bound on the sum of `obs_mask` on one device may be relied on, other than what follows from the above.
Results may differ from the reference program's by a relative error of at most 0.0065.
Values sent between devices are 32-bit elements; how exact they have to be, the bound alone decides.
A program may use at most 64 MiB of HBM per device.

```python
import math
import jax
import jax.numpy as jnp
from jax import lax

COLS = 4096
DATES = 16
ITERS = 2
LINES = 512


def draw_observed(key, part):
    first, second = jax.random.split(key)
    shape = (DATES, LINES, COLS)
    row_ids = lax.broadcasted_iota(jnp.int32, shape, 1).astype(jnp.float32)
    ramp = 1.0 + 2.0 * row_ids / max(LINES - 1, 1)
    rough = jnp.exp(jax.random.uniform(second, shape, jnp.float32, -0.7, 0.7))
    base = jnp.clip(jax.random.normal(first, shape, jnp.float32), -4.0, 4.0)
    return (base * ramp * rough).astype(jnp.float32)


def draw_inverse(key, part):
    first, second = jax.random.split(key)
    off = jax.random.uniform(first, (DATES, DATES, LINES, COLS), jnp.float32, -0.3, 0.3)
    sym = 0.5 * (off + jnp.swapaxes(off, 0, 1))
    diag = 5.0 + jax.random.uniform(second, (DATES, LINES, COLS), jnp.float32, 0.0, 2.0)
    eye = lax.broadcasted_iota(jnp.int32, (DATES, DATES, 1, 1), 0) == lax.broadcasted_iota(jnp.int32, (DATES, DATES, 1, 1), 1)
    full = jnp.where(eye, diag[:, None, :, :], sym)
    return full.astype(jnp.bfloat16)


def with_ends(values, stream_key, low, largest):
    shape = values.shape
    place = [jax.random.randint(jax.random.fold_in(stream_key, axis), (), 0, shape[axis]) for axis in range(len(shape))]
    values = values.at[tuple(place)].set(low)
    longest = shape.index(max(shape))
    place[longest] = (place[longest] + 1) % shape[longest]
    return values.at[tuple(place)].set(largest)


def shard_levels(stream_key, extent, cuts, low, top_value):
    def one(dim, blocks):
        steps = jax.random.uniform(jax.random.fold_in(jax.random.fold_in(stream_key, 6), dim), (blocks,), jnp.float32, low / len(cuts), top_value / len(cuts))
        return jnp.repeat(jnp.exp(steps), extent[dim] // blocks).reshape((-1,) + (1,) * (len(extent) - dim - 1))

    factor_of = one(*cuts[0])
    for cut in cuts[1:]:
        factor_of = factor_of * one(*cut)
    return factor_of


def setup_inputs(seed: int = 0) -> dict:
    streams_of = jax.random.split(jax.random.key(seed), 7)
    return {
        "obs_mask": with_ends((jax.random.randint(streams_of[0], (DATES, LINES, COLS), 0, 5) < 3).astype(jnp.int32), jax.random.fold_in(streams_of[0], 1), 0, 1),
        "precision": jnp.clip(jnp.exp(math.log(4.0) - 2.0794415 * jax.random.uniform(streams_of[1], (DATES, LINES, COLS), jnp.float32) ** shard_levels(streams_of[1], (DATES, LINES, COLS), ((0, 8), (1, 64)), -0.2, 0.2)), 0.5, 4.0),
        "observed": draw_observed(jax.random.fold_in(streams_of[6], 71), 0),
        "edge_class": with_ends(jax.random.randint(streams_of[3], (2, LINES, COLS), 0, 8), jax.random.fold_in(streams_of[3], 1), 0, 7).astype(jnp.int32),
        "temporal_weight": jnp.clip(jnp.exp(jax.random.uniform(streams_of[4], (DATES - 1,), jnp.float32, math.log(0.5), math.log(4.0))), 0.5, 4.0),
        "inverse": draw_inverse(jax.random.fold_in(streams_of[6], 71), 0),
    }


mass_term = 0.1


def edge_weights(edge_class, line_start, lines_total):
    classes = edge_class.astype(jnp.float32)
    rows_here = edge_class.shape[1]
    columns = edge_class.shape[2]
    col_ids = lax.broadcasted_iota(jnp.int32, (rows_here, columns), 1)
    row_ids = lax.broadcasted_iota(jnp.int32, (rows_here, columns), 0) + line_start
    across = jnp.where(col_ids == columns - 1, 0.0, 0.25 * (classes[0] + 1.0))
    downward = jnp.where(row_ids == lines_total - 1, 0.0, 0.25 * (classes[1] + 1.0))
    return across, downward


def operate(field, padded, data_weight, across, across_prev, downward, downward_prev, tau_up, tau_down):
    total = (mass_term + data_weight) * field
    total = total + across * (field - padded[1:-1, 1:-1, 2:]) + across_prev * (field - padded[1:-1, 1:-1, :-2])
    total = total + downward * (field - padded[1:-1, 2:, 1:-1]) + downward_prev * (field - padded[1:-1, :-2, 1:-1])
    total = total + tau_up * (field - padded[2:, 1:-1, 1:-1]) + tau_down * (field - padded[:-2, 1:-1, 1:-1])
    return total


def apply_inverse(inverse, values):
    total = inverse[:, 0].astype(jnp.float32) * values[0][None]
    for source in range(1, values.shape[0]):
        total = total + inverse[:, source].astype(jnp.float32) * values[source][None]
    return total


def reference(obs_mask, precision, observed, edge_class, temporal_weight, inverse):
    data_weight = obs_mask.astype(jnp.float32) * precision
    rhs = data_weight * observed
    across, downward = edge_weights(edge_class, 0, edge_class.shape[1])
    across_prev = jnp.pad(across, ((0, 0), (1, 0)))[:, :-1]
    downward_prev = jnp.pad(downward, ((1, 0), (0, 0)))[:-1]
    zero_one = jnp.zeros((1,), jnp.float32)
    tau_ext = jnp.concatenate([zero_one, temporal_weight, zero_one])
    tau_up = tau_ext[1:][:, None, None]
    tau_down = tau_ext[:-1][:, None, None]

    def operator(field):
        return operate(field, jnp.pad(field, 1), data_weight, across, across_prev, downward, downward_prev, tau_up, tau_down)

    solution = jnp.zeros_like(rhs)
    residual = rhs
    precond = apply_inverse(inverse, residual)
    search = precond
    rz_now = jnp.sum(residual * precond)
    for iteration in range(ITERS):
        image = operator(search)
        alpha = rz_now / jnp.sum(search * image)
        solution = solution + alpha * search
        residual = residual - alpha * image
        if iteration + 1 < ITERS:
            precond = apply_inverse(inverse, residual)
            rz_next = jnp.sum(residual * precond)
            search = precond + (rz_next / rz_now) * search
            rz_now = rz_next
    return solution, residual
```

```python
import jax
import jax.numpy as jnp
from jax import lax
from jax.sharding import PartitionSpec as P

mass_term = 0.1


def shifted(value, axis, steps):
    count = lax.axis_size(axis)
    first, last = (max(0, -steps), min(count, count - steps))
    return lax.ppermute(value, axis, [(i, i + steps) for i in range(first, last)])


def apply_inverse(inverse, values):
    total = inverse[:, 0].astype(jnp.float32) * values[0][None]
    for source in range(1, values.shape[0]):
        total = total + inverse[:, source].astype(jnp.float32) * values[source][None]
    return total


def body(obs_mask, precision, observed, edge_class, temporal_weight, inverse):
    dates_here, rows_here, columns = observed.shape
    cols_here = inverse.shape[3]
    line_start = lax.axis_index("rows") * rows_here
    lines_total = rows_here * lax.axis_size("rows")
    col_start = lax.axis_index("dates") * cols_here

    weight = obs_mask.astype(jnp.float32) * precision
    both = jnp.stack([weight, weight * observed])
    both = lax.all_to_all(both, "dates", split_axis=3, concat_axis=1, tiled=True)
    weight, rhs = both[0], both[1]

    classes = 0.25 * (edge_class.astype(jnp.float32) + 1.0)
    col_ids = lax.broadcasted_iota(jnp.int32, (rows_here, columns), 1)
    row_ids = lax.broadcasted_iota(jnp.int32, (rows_here, cols_here), 0) + line_start
    across_all = jnp.where(col_ids == columns - 1, 0.0, classes[0])
    across_ext = jnp.pad(across_all, ((0, 0), (1, 0)))
    across_prev = lax.dynamic_slice_in_dim(across_ext, col_start, cols_here, 1)
    across = lax.dynamic_slice_in_dim(across_all, col_start, cols_here, 1)
    downward = lax.dynamic_slice_in_dim(classes[1], col_start, cols_here, 1)
    downward = jnp.where(row_ids == lines_total - 1, 0.0, downward)
    downward_prev = jnp.concatenate([shifted(downward[-1:], "rows", 1), downward[:-1]], axis=0)
    zero_one = jnp.zeros((1,), jnp.float32)
    tau_up = jnp.concatenate([temporal_weight, zero_one])[:, None, None]
    tau_down = jnp.concatenate([zero_one, temporal_weight])[:, None, None]
    centre = (
        mass_term + weight + (across + across_prev + downward + downward_prev)[None]
        + (tau_up + tau_down)
    )

    def operator(field):
        above = jnp.concatenate([shifted(field[:, -1:], "rows", 1), field[:, :-1]], axis=1)
        below = jnp.concatenate([field[:, 1:], shifted(field[:, :1], "rows", -1)], axis=1)
        left = jnp.concatenate([shifted(field[:, :, -1:], "dates", 1), field[:, :, :-1]], axis=2)
        right = jnp.concatenate([field[:, :, 1:], shifted(field[:, :, :1], "dates", -1)], axis=2)
        before = jnp.pad(field, ((1, 0), (0, 0), (0, 0)))[:-1]
        after = jnp.pad(field, ((0, 1), (0, 0), (0, 0)))[1:]
        return (
            centre * field
            - (across * right + across_prev * left)
            - (downward * below + downward_prev * above)
            - (tau_up * after + tau_down * before)
        )

    precond = apply_inverse(inverse, rhs)
    image = operator(precond)
    mapped = apply_inverse(inverse, image)
    mapped_image = operator(mapped)
    sums = jnp.stack(
        [
            jnp.sum(rhs * precond),
            jnp.sum(precond * image),
            jnp.sum(image * mapped),
            jnp.sum(mapped * mapped_image),
        ]
    )
    sums = lax.psum(sums, ("rows", "dates"))
    rz, dd, ee, ff = sums[0], sums[1], sums[2], sums[3]
    alpha = rz / dd
    grown = alpha * ee / dd
    alpha_next = (alpha * alpha * ee - rz) / (alpha * alpha * (ff - ee * ee / dd))
    first = alpha + alpha_next * grown
    second = alpha_next * alpha
    out = jnp.stack([first * precond - second * mapped, rhs - first * image + second * mapped_image])
    out = lax.all_to_all(out, "dates", split_axis=1, concat_axis=3, tiled=True)
    return out[0], out[1]


def solution(mesh):
    return jax.shard_map(
        body,
        mesh=mesh,
        in_specs=(
            P("dates", "rows", None),
            P("dates", "rows", None),
            P("dates", "rows", None),
            P(None, "rows", None),
            P(),
            P(None, None, "rows", "dates"),
        ),
        out_specs=(P("dates", "rows", None), P("dates", "rows", None)),
        check_vma=False,
    )
```

```python
import functools
import jax
import jax.numpy as jnp
from jax import lax
from jax.experimental import pallas as pl
from jax.experimental.pallas import tpu as pltpu
from jax.sharding import PartitionSpec as P

MASS = 0.1
LANES = 128
UNROLL = 4
MESH = pl.DeviceIdType.MESH
RHS, WEIGHT, PRECOND, MAPPED, RESIDUAL = range(5)


def kernel(
    rows, groups, low_size,
    mask_hbm, prec_hbm, obs_hbm, edge_hbm, tau_ref, inv_hbm,
    sol_ref, res_ref,
    mask, prec, obs, edge, inv,
    weight_date, rhs_date, precond_date, mapped_date, residual_date,
    weight, rhs, precond, image, mapped, second_image, residual,
    across, across_prev, downward, downward_prev,
    down_send, up_send, from_above, from_below,
    right_send, left_send, from_left, from_right,
    part, parts,
    local_sem, send_sem, recv_sem, halo_send_sem, halo_recv_sem, sum_send_sem, sum_recv_sem,
):
    dates_here, height, columns = mask.shape
    dates, _, width = rhs.shape
    row = lax.axis_index("rows")
    group = lax.axis_index("dates")
    low, high = row % low_size, row // low_size
    high_size = rows // low_size
    above_row, below_row = (row + rows - 1) % rows, (row + 1) % rows
    left_group, right_group = (group + groups - 1) % groups, (group + 1) % groups
    my_columns = pl.ds(pl.multiple_of(group * width, width), width)

    def sum_peer(phase, step):
        if phase == 0:
            return (row, (group + step) % groups)
        if phase == 1:
            return (high * low_size + (low + step) % low_size, group)
        return (((high + step) % high_size) * low_size + low, group)

    phases = ((groups, group), (low_size, low), (high_size, high))

    barrier = pltpu.get_barrier_semaphore()
    greeted = 0
    for phase, (size, _) in enumerate(phases):
        for step in range(1, size):
            pl.semaphore_signal(
                barrier, inc=1, device_id=sum_peer(phase, step), device_id_type=MESH
            )
            greeted += 1
    for neighbour in (above_row, below_row):
        pl.semaphore_signal(barrier, inc=1, device_id=(neighbour, group), device_id_type=MESH)
        greeted += 1

    loads = [
        pltpu.make_async_copy(source, target, local_sem.at[number])
        for number, (source, target) in enumerate(
            ((mask_hbm, mask), (prec_hbm, prec), (obs_hbm, obs), (edge_hbm, edge), (inv_hbm, inv))
        )
    ]
    for load in loads:
        load.start()

    for load in loads[:3]:
        load.wait()
    for date in range(dates_here):
        here = mask[date].astype(jnp.float32) * prec[date]
        weight_date[date] = here
        rhs_date[date] = here * obs[date]
    for date in range(dates_here):
        rhs[group * dates_here + date] = rhs_date[date, :, my_columns]
        weight[group * dates_here + date] = weight_date[date, :, my_columns]
    pl.semaphore_wait(barrier, greeted)

    def inward(field, source, target, step):
        peer = (group + step) % groups
        came_from = (group + groups - step) % groups
        block = source.at[:, :, pl.ds(pl.multiple_of(peer * width, width), width)]
        sent = pltpu.make_async_remote_copy(
            block, target.at[pl.ds(group * dates_here, dates_here)],
            send_sem.at[field, peer], recv_sem.at[field, group], (row, peer), MESH,
        )
        got = pltpu.make_async_remote_copy(
            block, target.at[pl.ds(came_from * dates_here, dates_here)],
            send_sem.at[field, peer], recv_sem.at[field, came_from], (row, peer), MESH,
        )
        return sent, got

    def outward(field, source, first, target, step):
        peer = (group + step) % groups
        came_from = (group + groups - step) % groups
        block = source.at[pl.ds(first + peer * dates_here, dates_here)]
        sent = pltpu.make_async_remote_copy(
            block, target.at[:, :, my_columns],
            send_sem.at[field, peer], recv_sem.at[field, group], (row, peer), MESH,
        )
        got = pltpu.make_async_remote_copy(
            block, target.at[:, :, pl.ds(pl.multiple_of(came_from * width, width), width)],
            send_sem.at[field, peer], recv_sem.at[field, came_from], (row, peer), MESH,
        )
        return sent, got

    half = groups // 2
    steps = sorted(range(1, groups), key=lambda step: (-min(step, groups - step), step))
    assert half >= 1
    rhs_copies = [inward(RHS, rhs_date, rhs, step) for step in steps]
    weight_copies = [inward(WEIGHT, weight_date, weight, step) for step in steps]
    for sent, _ in rhs_copies:
        sent.start()
    for sent, _ in weight_copies:
        sent.start()

    loads[3].wait()
    lane = lax.broadcasted_iota(jnp.int32, (height, LANES), 1)
    col = lax.broadcasted_iota(jnp.int32, (height, width), 1)
    line = lax.broadcasted_iota(jnp.int32, (height, width), 0)
    steps_across = 0.25 * (edge[0, :, my_columns].astype(jnp.float32) + 1.0)
    steps_down = 0.25 * (edge[1, :, my_columns].astype(jnp.float32) + 1.0)
    across[...] = jnp.where((col == width - 1) & (group == groups - 1), 0.0, steps_across)
    before = (left_group + 1) * width - LANES
    edge_before = edge[0, :, pl.ds(pl.multiple_of(before, LANES), LANES)].astype(jnp.float32)
    edge_before = pltpu.roll(0.25 * (edge_before + 1.0), 1, 1)
    edge_before = jnp.where(group == 0, 0.0, edge_before)

    def with_first(block, tile):
        first = jnp.where(lane == 0, tile, block[:, :LANES])
        if width == LANES:
            return first
        return jnp.concatenate([first, block[:, LANES:]], axis=1)

    def with_last(block, tile):
        last = jnp.where(lane == LANES - 1, tile, block[:, width - LANES :])
        if width == LANES:
            return last
        return jnp.concatenate([block[:, : width - LANES], last], axis=1)

    across_prev[...] = with_first(pltpu.roll(steps_across, 1, 1), edge_before)
    down_here = jnp.where((line == height - 1) & (row == rows - 1), 0.0, steps_down)
    downward[...] = down_here
    down_send[0, dates:, :] = jnp.broadcast_to(
        down_here[height - 1 :, :], (down_send.shape[1] - dates, width)
    )
    down_send[1, dates:, :] = jnp.zeros((down_send.shape[1] - dates, width), jnp.float32)
    for field in (precond, mapped):
        field[0] = jnp.zeros((height, width), jnp.float32)
        field[dates + 1] = jnp.zeros((height, width), jnp.float32)

    def folded(block):
        total = block[:, :LANES]
        for start in range(LANES, width, LANES):
            total = total + block[:, start : start + LANES]
        return total

    def over_dates(step_of, init):
        def several(index, carry):
            for inner in range(UNROLL):
                carry = step_of(index * UNROLL + inner, carry)
            return carry

        return lax.fori_loop(0, dates // UNROLL, several, init)

    none = jnp.zeros((height, LANES), jnp.float32)

    def precondition(source, target, turn):
        def one(date, carry):
            total, to_right, to_left = carry
            out = inv[date, 0].astype(jnp.float32) * source[0]
            for other in range(1, dates):
                out = out + inv[date, other].astype(jnp.float32) * source[other]
            target[date + 1] = out
            down_send[turn, pl.ds(date, 1), :] = out[height - 1 :, :]
            up_send[turn, pl.ds(date, 1), :] = out[:1, :]
            to_right = jnp.where(
                lane == date, pltpu.roll(out[:, width - LANES :], date + 1, 1), to_right
            )
            to_left = jnp.where(lane == date, pltpu.roll(out[:, :LANES], date, 1), to_left)
            return total + folded(source[date] * out), to_right, to_left

        total, to_right, to_left = over_dates(one, (none, none, none))
        right_send[turn] = to_right
        left_send[turn] = to_left
        return total

    def halo(turn):
        pairs = (
            (down_send, from_above, (below_row, group)),
            (up_send, from_below, (above_row, group)),
            (right_send, from_left, (row, right_group)),
            (left_send, from_right, (row, left_group)),
        )
        return [
            pltpu.make_async_remote_copy(
                source.at[turn], target.at[turn],
                halo_send_sem.at[turn, number], halo_recv_sem.at[turn, number], device, MESH,
            )
            for number, (source, target, device) in enumerate(pairs)
        ]

    def operator(field, target, turn):
        def one(date, total):
            here = field[date + 1]
            above = jnp.where(
                line == 0, from_above[turn, pl.ds(date, 1), :], pltpu.roll(here, 1, 0)
            )
            below = jnp.where(
                line == height - 1,
                from_below[turn, pl.ds(date, 1), :],
                pltpu.roll(here, height - 1, 0),
            )
            left = with_first(
                pltpu.roll(here, 1, 1),
                pltpu.roll(from_left[turn], (LANES - date) % LANES, 1),
            )
            right = with_last(
                pltpu.roll(here, width - 1, 1),
                pltpu.roll(from_right[turn], LANES - 1 - date, 1),
            )
            out = (MASS + weight[date]) * here
            out = out + across[...] * (here - right) + across_prev[...] * (here - left)
            out = out + downward[...] * (here - below) + downward_prev[...] * (here - above)
            out = out + tau_ref[date + 1] * (here - field[date + 2])
            out = out + tau_ref[date] * (here - field[date])
            target[date] = out
            return total + folded(here * out)

        return over_dates(one, none)

    def bring_back(field, source, target):
        copies = [outward(field, source, 1, target, step) for step in steps]
        for sent, _ in copies:
            sent.start()
        for date in range(dates_here):
            target[date, :, my_columns] = source[1 + group * dates_here + date]
        return copies

    loads[4].wait()
    for _, got in rhs_copies:
        got.wait_recv()
    sum_rz = precondition(rhs, precond, 0)
    first_halo = halo(0)
    for copy in first_halo:
        copy.start()
    precond_copies = bring_back(PRECOND, precond, precond_date)
    for _, got in weight_copies:
        got.wait_recv()
    for copy in first_halo:
        copy.wait_recv()
    downward_prev[...] = jnp.where(
        line == 0,
        jnp.where(row == 0, 0.0, from_above[0, dates : dates + 1, :]),
        pltpu.roll(downward[...], 1, 0),
    )
    sum_d = operator(precond, image, 0)
    sum_e = precondition(image, mapped, 1)
    second_halo = halo(1)
    for copy in second_halo:
        copy.start()
    mapped_copies = bring_back(MAPPED, mapped, mapped_date)
    for copy in second_halo:
        copy.wait_recv()
    sum_f = operator(mapped, second_image, 1)

    tile_line = lax.broadcasted_iota(jnp.int32, (height, LANES), 0)
    tile = jnp.zeros((height, LANES), jnp.float32)
    for number, total in enumerate((sum_rz, sum_d, sum_e, sum_f)):
        tile = jnp.where(tile_line == number, jnp.sum(total, axis=0, keepdims=True), tile)
    sum_copies = []
    for phase, (size, mine) in enumerate(phases):
        part[phase] = tile
        parts[phase, mine] = tile
        received = []
        for step in range(1, size):
            came_from = (mine + size - step) % size
            sent = pltpu.make_async_remote_copy(
                part.at[phase], parts.at[phase, mine],
                sum_send_sem.at[phase, step], sum_recv_sem.at[phase, mine],
                sum_peer(phase, step), MESH,
            )
            sent.start()
            sum_copies.append(sent)
            received.append(
                pltpu.make_async_remote_copy(
                    part.at[phase], parts.at[phase, came_from],
                    sum_send_sem.at[phase, step], sum_recv_sem.at[phase, came_from],
                    sum_peer(phase, step), MESH,
                )
            )
        for got in received:
            got.wait_recv()
        tile = parts[phase, 0]
        for other in range(1, size):
            tile = tile + parts[phase, other]
    lines = jnp.sum(tile, axis=1, keepdims=True)
    rz, dd, ee, ff = (lines[number : number + 1] for number in range(4))
    alpha = rz / dd
    grown = alpha * ee / dd
    alpha_next = (alpha * alpha * ee - rz) / (alpha * alpha * (ff - ee * ee / dd))
    first = alpha + alpha_next * grown
    second = alpha_next * alpha
    first = jnp.broadcast_to(first, (height, width))
    second = jnp.broadcast_to(second, (height, width))

    def finish(date, carry):
        residual[date + 1] = rhs[date] - first * image[date] + second * second_image[date]
        return carry

    over_dates(finish, 0)
    residual_copies = bring_back(RESIDUAL, residual, residual_date)
    for copies in (precond_copies, mapped_copies):
        for _, got in copies:
            got.wait_recv()
    for date in range(dates_here):
        for number in range(groups):
            part_of = slice(number * width, (number + 1) * width)
            sol_ref[date, :, part_of] = (
                first * precond_date[date, :, part_of] - second * mapped_date[date, :, part_of]
            )
    for _, got in residual_copies:
        got.wait_recv()
    res_ref[...] = residual_date[...]
    for copies in (rhs_copies, weight_copies, precond_copies, mapped_copies, residual_copies):
        for sent, _ in copies:
            sent.wait_send()
    for copy in first_halo + second_halo + sum_copies:
        copy.wait_send()


def body(obs_mask, precision, observed, edge_class, temporal_weight, inverse):
    rows, groups = lax.axis_size("rows"), lax.axis_size("dates")
    low_size = 8 if rows >= 64 else 2
    dates, _, height, width = inverse.shape
    zero_one = jnp.zeros((1,), jnp.float32)
    tau = jnp.concatenate([zero_one, temporal_weight, zero_one])
    f32 = jnp.float32
    whole = observed.shape
    block = (dates, height, width)
    padded = (dates + 2, height, width)
    most = max(groups, low_size, rows // low_size)
    vmem = pltpu.VMEM
    dma = pltpu.SemaphoreType.DMA
    scratch = (
        [vmem(whole, jnp.int32), vmem(whole, f32), vmem(whole, f32)]
        + [vmem(edge_class.shape, jnp.int32), vmem(inverse.shape, jnp.bfloat16)]
        + [vmem(whole, f32)] * 5
        + [vmem(block, f32), vmem(block, f32), vmem(padded, f32), vmem(block, f32)]
        + [vmem(padded, f32), vmem(block, f32), vmem(padded, f32)]
        + [vmem((height, width), f32)] * 4
        + [vmem((2, dates + 8, width), f32), vmem((2, dates, width), f32)] * 2
        + [vmem((2, height, LANES), f32)] * 4
        + [vmem((3, height, LANES), f32), vmem((3, most, height, LANES), f32)]
        + [dma((5,)), dma((5, groups)), dma((5, groups)), dma((2, 4)), dma((2, 4))]
        + [dma((3, most)), dma((3, most))]
    )
    anywhere = pl.BlockSpec(memory_space=pl.ANY)
    return pl.pallas_call(
        functools.partial(kernel, rows, groups, low_size),
        out_shape=[jax.ShapeDtypeStruct(whole, f32)] * 2,
        in_specs=[anywhere] * 4 + [pl.BlockSpec(memory_space=pltpu.SMEM), anywhere],
        out_specs=[pl.BlockSpec(memory_space=pltpu.VMEM)] * 2,
        scratch_shapes=scratch,
        compiler_params=pltpu.CompilerParams(collective_id=0, has_side_effects=True),
        name="cg",
    )(obs_mask, precision, observed, edge_class, tau, inverse)


def solution(mesh):
    return jax.shard_map(
        body,
        mesh=mesh,
        in_specs=(
            P("dates", "rows", None),
            P("dates", "rows", None),
            P("dates", "rows", None),
            P(None, "rows", None),
            P(),
            P(None, None, "rows", "dates"),
        ),
        out_specs=(P("dates", "rows", None), P("dates", "rows", None)),
        check_vma=False,
    )
```

```python
import functools
import jax
import jax.numpy as jnp
from jax import lax
from jax.experimental import pallas as pl
from jax.experimental.pallas import tpu as pltpu
from jax.sharding import PartitionSpec as P

MASS = 0.1
LANES = 128
UNROLL = 4
VMEM_BYTES = 16 * 1024 * 1024
MESH = pl.DeviceIdType.MESH
RHS, WEIGHT, PRECOND, IMAGE, MAPPED, SECOND = range(6)


def kernel(
    rows, groups, low_size,
    mask_hbm, prec_hbm, obs_hbm, edge_hbm, tau_ref, inv_hbm,
    sol_ref, res_ref,
    mask, prec, obs, edge, inv,
    weight_date, rhs_date, precond_date, image_date, mapped_date, second_date,
    weight, rhs, precond, image, mapped, second_image,
    across, across_prev, downward, downward_prev,
    down_send, up_send, from_above, from_below,
    right_send, left_send, from_left, from_right,
    part, parts,
    local_sem, send_sem, recv_sem, halo_send_sem, halo_recv_sem, sum_send_sem, sum_recv_sem,
):
    dates_here, height, columns = mask.shape
    dates, _, width = rhs.shape
    row = lax.axis_index("rows")
    group = lax.axis_index("dates")
    low, high = row % low_size, row // low_size
    high_size = rows // low_size
    above_row, below_row = (row + rows - 1) % rows, (row + 1) % rows
    left_group, right_group = (group + groups - 1) % groups, (group + 1) % groups
    my_columns = pl.ds(pl.multiple_of(group * width, width), width)

    def sum_peer(phase, step):
        if phase == 0:
            return (high * low_size + (low + step) % low_size, group)
        if phase == 1:
            return (((high + step) % high_size) * low_size + low, group)
        return (row, (group + step) % groups)

    phases = ((low_size, low), (high_size, high), (groups, group))

    barrier = pltpu.get_barrier_semaphore()
    greeted = 0
    for phase, (size, _) in enumerate(phases):
        for step in range(1, size):
            pl.semaphore_signal(
                barrier, inc=1, device_id=sum_peer(phase, step), device_id_type=MESH
            )
            greeted += 1
    for neighbour in (above_row, below_row):
        pl.semaphore_signal(barrier, inc=1, device_id=(neighbour, group), device_id_type=MESH)
        greeted += 1

    loads = [
        pltpu.make_async_copy(source, target, local_sem.at[number])
        for number, (source, target) in enumerate(
            ((mask_hbm, mask), (prec_hbm, prec), (obs_hbm, obs), (edge_hbm, edge), (inv_hbm, inv))
        )
    ]
    for load in loads:
        load.start()

    for load in loads[:3]:
        load.wait()
    for date in range(dates_here):
        here = mask[date].astype(jnp.float32) * prec[date]
        weight_date[date] = here
        rhs_date[date] = here * obs[date]
    for date in range(dates_here):
        rhs[group * dates_here + date] = rhs_date[date, :, my_columns]
        weight[group * dates_here + date] = weight_date[date, :, my_columns]
    pl.semaphore_wait(barrier, greeted)

    def inward(field, source, target, step):
        peer = (group + step) % groups
        came_from = (group + groups - step) % groups
        block = source.at[:, :, pl.ds(pl.multiple_of(peer * width, width), width)]
        sent = pltpu.make_async_remote_copy(
            block, target.at[pl.ds(group * dates_here, dates_here)],
            send_sem.at[field, peer], recv_sem.at[field, group], (row, peer), MESH,
        )
        got = pltpu.make_async_remote_copy(
            block, target.at[pl.ds(came_from * dates_here, dates_here)],
            send_sem.at[field, peer], recv_sem.at[field, came_from], (row, peer), MESH,
        )
        return sent, got

    def outward(field, source, first, target, step):
        peer = (group + step) % groups
        came_from = (group + groups - step) % groups
        block = source.at[pl.ds(first + peer * dates_here, dates_here)]
        sent = pltpu.make_async_remote_copy(
            block, target.at[:, :, my_columns],
            send_sem.at[field, peer], recv_sem.at[field, group], (row, peer), MESH,
        )
        got = pltpu.make_async_remote_copy(
            block, target.at[:, :, pl.ds(pl.multiple_of(came_from * width, width), width)],
            send_sem.at[field, peer], recv_sem.at[field, came_from], (row, peer), MESH,
        )
        return sent, got

    half = groups // 2
    steps = sorted(range(1, groups), key=lambda step: (-min(step, groups - step), step))
    assert half >= 1
    rhs_copies = [inward(RHS, rhs_date, rhs, step) for step in steps]
    weight_copies = [inward(WEIGHT, weight_date, weight, step) for step in steps]
    for sent, _ in rhs_copies:
        sent.start()
    for sent, _ in weight_copies:
        sent.start()

    loads[3].wait()
    lane = lax.broadcasted_iota(jnp.int32, (height, LANES), 1)
    col = lax.broadcasted_iota(jnp.int32, (height, width), 1)
    line = lax.broadcasted_iota(jnp.int32, (height, width), 0)
    steps_across = 0.25 * (edge[0, :, my_columns].astype(jnp.float32) + 1.0)
    steps_down = 0.25 * (edge[1, :, my_columns].astype(jnp.float32) + 1.0)
    across[...] = jnp.where((col == width - 1) & (group == groups - 1), 0.0, steps_across)
    before = (left_group + 1) * width - LANES
    edge_before = edge[0, :, pl.ds(pl.multiple_of(before, LANES), LANES)].astype(jnp.float32)
    edge_before = pltpu.roll(0.25 * (edge_before + 1.0), 1, 1)
    edge_before = jnp.where(group == 0, 0.0, edge_before)

    def with_first(block, tile):
        first = jnp.where(lane == 0, tile, block[:, :LANES])
        if width == LANES:
            return first
        return jnp.concatenate([first, block[:, LANES:]], axis=1)

    def with_last(block, tile):
        last = jnp.where(lane == LANES - 1, tile, block[:, width - LANES :])
        if width == LANES:
            return last
        return jnp.concatenate([block[:, : width - LANES], last], axis=1)

    across_prev[...] = with_first(pltpu.roll(steps_across, 1, 1), edge_before)
    down_here = jnp.where((line == height - 1) & (row == rows - 1), 0.0, steps_down)
    downward[...] = down_here
    down_send[0, dates:, :] = jnp.broadcast_to(
        down_here[height - 1 :, :], (down_send.shape[1] - dates, width)
    )
    down_send[1, dates:, :] = jnp.zeros((down_send.shape[1] - dates, width), jnp.float32)
    for field in (precond, mapped):
        field[0] = jnp.zeros((height, width), jnp.float32)
        field[dates + 1] = jnp.zeros((height, width), jnp.float32)

    def folded(block):
        total = block[:, :LANES]
        for start in range(LANES, width, LANES):
            total = total + block[:, start : start + LANES]
        return total

    def over_dates(step_of, init):
        def several(index, carry):
            for inner in range(UNROLL):
                carry = step_of(index * UNROLL + inner, carry)
            return carry

        return lax.fori_loop(0, dates // UNROLL, several, init)

    none = jnp.zeros((height, LANES), jnp.float32)

    def precondition(source, target, turn):
        def one(date, carry):
            total, to_right, to_left = carry
            out = inv[date, 0].astype(jnp.float32) * source[0]
            for other in range(1, dates):
                out = out + inv[date, other].astype(jnp.float32) * source[other]
            target[date + 1] = out
            down_send[turn, pl.ds(date, 1), :] = out[height - 1 :, :]
            up_send[turn, pl.ds(date, 1), :] = out[:1, :]
            to_right = jnp.where(
                lane == date, pltpu.roll(out[:, width - LANES :], date + 1, 1), to_right
            )
            to_left = jnp.where(lane == date, pltpu.roll(out[:, :LANES], date, 1), to_left)
            return total + folded(source[date] * out), to_right, to_left

        total, to_right, to_left = over_dates(one, (none, none, none))
        right_send[turn] = to_right
        left_send[turn] = to_left
        return total

    def halo(turn):
        pairs = (
            (down_send, from_above, (below_row, group)),
            (up_send, from_below, (above_row, group)),
            (right_send, from_left, (row, right_group)),
            (left_send, from_right, (row, left_group)),
        )
        return [
            pltpu.make_async_remote_copy(
                source.at[turn], target.at[turn],
                halo_send_sem.at[turn, number], halo_recv_sem.at[turn, number], device, MESH,
            )
            for number, (source, target, device) in enumerate(pairs)
        ]

    def operator(field, target, turn):
        def one(date, total):
            here = field[date + 1]
            above = jnp.where(
                line == 0, from_above[turn, pl.ds(date, 1), :], pltpu.roll(here, 1, 0)
            )
            below = jnp.where(
                line == height - 1,
                from_below[turn, pl.ds(date, 1), :],
                pltpu.roll(here, height - 1, 0),
            )
            left = with_first(
                pltpu.roll(here, 1, 1),
                pltpu.roll(from_left[turn], (LANES - date) % LANES, 1),
            )
            right = with_last(
                pltpu.roll(here, width - 1, 1),
                pltpu.roll(from_right[turn], LANES - 1 - date, 1),
            )
            tau_up = jnp.where(date < dates - 1, tau_ref[jnp.minimum(date, dates - 2)], 0.0)
            tau_down = jnp.where(date > 0, tau_ref[jnp.maximum(date - 1, 0)], 0.0)
            out = (MASS + weight[date]) * here
            out = out + across[...] * (here - right) + across_prev[...] * (here - left)
            out = out + downward[...] * (here - below) + downward_prev[...] * (here - above)
            out = out + tau_up * (here - field[date + 2])
            out = out + tau_down * (here - field[date])
            target[date] = out
            return total + folded(here * out)

        return over_dates(one, none)

    def bring_back(field, source, first, target):
        copies = [outward(field, source, first, target, step) for step in steps]
        for sent, _ in copies:
            sent.start()
        for date in range(dates_here):
            target[date, :, my_columns] = source[first + group * dates_here + date]
        return copies

    loads[4].wait()
    for _, got in rhs_copies:
        got.wait_recv()
    sum_rz = precondition(rhs, precond, 0)
    first_halo = halo(0)
    for copy in first_halo:
        copy.start()
    precond_copies = bring_back(PRECOND, precond, 1, precond_date)
    for _, got in weight_copies:
        got.wait_recv()
    for copy in first_halo:
        copy.wait_recv()
    downward_prev[...] = jnp.where(
        line == 0,
        jnp.where(row == 0, 0.0, from_above[0, dates : dates + 1, :]),
        pltpu.roll(downward[...], 1, 0),
    )
    sum_d = operator(precond, image, 0)
    image_copies = bring_back(IMAGE, image, 0, image_date)
    sum_e = precondition(image, mapped, 1)
    second_halo = halo(1)
    for copy in second_halo:
        copy.start()
    mapped_copies = bring_back(MAPPED, mapped, 1, mapped_date)
    for copy in second_halo:
        copy.wait_recv()
    sum_f = operator(mapped, second_image, 1)
    second_copies = bring_back(SECOND, second_image, 0, second_date)

    tile_line = lax.broadcasted_iota(jnp.int32, (height, LANES), 0)
    tile = jnp.zeros((height, LANES), jnp.float32)
    for number, total in enumerate((sum_rz, sum_d, sum_e, sum_f)):
        tile = jnp.where(tile_line == number, jnp.sum(total, axis=0, keepdims=True), tile)
    sum_copies = []
    for phase, (size, mine) in enumerate(phases):
        part[phase] = tile
        parts[phase, mine] = tile
        received = []
        for step in range(1, size):
            came_from = (mine + size - step) % size
            sent = pltpu.make_async_remote_copy(
                part.at[phase], parts.at[phase, mine],
                sum_send_sem.at[phase, step], sum_recv_sem.at[phase, mine],
                sum_peer(phase, step), MESH,
            )
            sent.start()
            sum_copies.append(sent)
            received.append(
                pltpu.make_async_remote_copy(
                    part.at[phase], parts.at[phase, came_from],
                    sum_send_sem.at[phase, step], sum_recv_sem.at[phase, came_from],
                    sum_peer(phase, step), MESH,
                )
            )
        for got in received:
            got.wait_recv()
        tile = parts[phase, 0]
        for other in range(1, size):
            tile = tile + parts[phase, other]
    lines = jnp.sum(tile, axis=1, keepdims=True)
    rz, dd, ee, ff = (lines[number : number + 1] for number in range(4))
    alpha = rz / dd
    grown = alpha * ee / dd
    alpha_next = (alpha * alpha * ee - rz) / (alpha * alpha * (ff - ee * ee / dd))
    first = alpha + alpha_next * grown
    second = alpha_next * alpha
    first = jnp.broadcast_to(first, (height, width))
    second = jnp.broadcast_to(second, (height, width))

    def whole_row(output, combine, *copied):
        for copies in copied:
            for _, got in copies:
                got.wait_recv()
        for date in range(dates_here):
            for number in range(groups):
                output[date, :, number * width : (number + 1) * width] = combine(
                    (date, slice(None), slice(number * width, (number + 1) * width))
                )

    whole_row(
        sol_ref,
        lambda at: first * precond_date[at] - second * mapped_date[at],
        precond_copies, mapped_copies,
    )
    whole_row(
        res_ref,
        lambda at: rhs_date[at] - first * image_date[at] + second * second_date[at],
        image_copies, second_copies,
    )
    back = (precond_copies, image_copies, mapped_copies, second_copies)
    for copies in (rhs_copies, weight_copies) + back:
        for sent, _ in copies:
            sent.wait_send()
    for copy in first_halo + second_halo + sum_copies:
        copy.wait_send()


def body(obs_mask, precision, observed, edge_class, temporal_weight, inverse):
    rows, groups = lax.axis_size("rows"), lax.axis_size("dates")
    low_size = 8 if rows >= 64 else 2
    dates, _, height, width = inverse.shape
    f32 = jnp.float32
    whole = observed.shape
    block = (dates, height, width)
    padded = (dates + 2, height, width)
    most = max(groups, low_size, rows // low_size)
    vmem = pltpu.VMEM
    dma = pltpu.SemaphoreType.DMA
    scratch = (
        [vmem(whole, jnp.int32), vmem(whole, f32), vmem(whole, f32)]
        + [vmem(edge_class.shape, jnp.int32), vmem(inverse.shape, jnp.bfloat16)]
        + [vmem(whole, f32)] * 6
        + [vmem(block, f32), vmem(block, f32), vmem(padded, f32), vmem(block, f32)]
        + [vmem(padded, f32), vmem(block, f32)]
        + [vmem((height, width), f32)] * 4
        + [vmem((2, dates + 8, width), f32), vmem((2, dates, width), f32)] * 2
        + [vmem((2, height, LANES), f32)] * 4
        + [vmem((3, height, LANES), f32), vmem((3, most, height, LANES), f32)]
        + [dma((5,)), dma((6, groups)), dma((6, groups)), dma((2, 4)), dma((2, 4))]
        + [dma((3, most)), dma((3, most))]
    )
    anywhere = pl.BlockSpec(memory_space=pltpu.HBM)
    return pl.pallas_call(
        functools.partial(kernel, rows, groups, low_size),
        out_shape=[jax.ShapeDtypeStruct(whole, f32)] * 2,
        in_specs=[anywhere] * 4 + [pl.BlockSpec(memory_space=pltpu.SMEM), anywhere],
        out_specs=[pl.BlockSpec(memory_space=pltpu.VMEM)] * 2,
        scratch_shapes=scratch,
        compiler_params=pltpu.CompilerParams(collective_id=0, has_side_effects=True, vmem_limit_bytes=VMEM_BYTES),
        name="cg",
    )(obs_mask, precision, observed, edge_class, temporal_weight, inverse)


def solution(mesh):
    return jax.shard_map(
        body,
        mesh=mesh,
        in_specs=(
            P("dates", "rows", None),
            P("dates", "rows", None),
            P("dates", "rows", None),
            P(None, "rows", None),
            P(),
            P(None, None, "rows", "dates"),
        ),
        out_specs=(P("dates", "rows", None), P("dates", "rows", None)),
        check_vma=False,
    )
```

```python
import functools
import jax
import jax.numpy as jnp
from jax import lax
from jax.experimental import pallas as pl
from jax.experimental.pallas import tpu as pltpu
from jax.sharding import PartitionSpec as P

MASS = 0.1
LANES = 128
UNROLL = 4
VMEM_BYTES = 16 * 1024 * 1024
MESH = pl.DeviceIdType.MESH
RHS, WEIGHT, PRECOND, IMAGE, MAPPED, SECOND = range(6)


def kernel(
    rows, groups, low_size,
    mask_hbm, prec_hbm, obs_hbm, edge_hbm, tau_hbm, inv_hbm,
    sol_ref, res_ref,
    mask, prec, obs, edge, inv,
    weight_date, rhs_date, precond_date, image_date, mapped_date, second_date,
    weight, rhs, precond, image, mapped, second_image,
    across, across_prev, downward, downward_prev,
    down_send, up_send, from_above, from_below,
    right_send, left_send, from_left, from_right,
    part, parts,
    tau_ref, local_sem, send_sem, recv_sem, halo_send_sem, halo_recv_sem, sum_send_sem, sum_recv_sem,
):
    dates_here, height, columns = mask.shape
    dates, _, width = rhs.shape
    row = lax.axis_index("rows")
    group = lax.axis_index("dates")
    low, high = row % low_size, row // low_size
    high_size = rows // low_size
    above_row, below_row = (row + rows - 1) % rows, (row + 1) % rows
    left_group, right_group = (group + groups - 1) % groups, (group + 1) % groups
    my_columns = pl.ds(pl.multiple_of(group * width, width), width)

    def sum_peer(phase, step):
        if phase == 0:
            return (row, (group + step) % groups)
        if phase == 1:
            return (high * low_size + (low + step) % low_size, group)
        return (((high + step) % high_size) * low_size + low, group)

    phases = ((groups, group), (low_size, low), (high_size, high))

    barrier = pltpu.get_barrier_semaphore()
    greeted = 0
    for phase, (size, _) in enumerate(phases):
        for step in range(1, size):
            pl.semaphore_signal(
                barrier, inc=1, device_id=sum_peer(phase, step), device_id_type=MESH
            )
            greeted += 1
    for neighbour in (above_row, below_row):
        pl.semaphore_signal(barrier, inc=1, device_id=(neighbour, group), device_id_type=MESH)
        greeted += 1

    loads = [
        pltpu.make_async_copy(source, target, local_sem.at[number])
        for number, (source, target) in enumerate(
            ((mask_hbm, mask), (prec_hbm, prec), (obs_hbm, obs), (edge_hbm, edge), (inv_hbm, inv), (tau_hbm, tau_ref))
        )
    ]
    for load in loads:
        load.start()

    for load in loads[:3]:
        load.wait()
    for date in range(dates_here):
        here = mask[date].astype(jnp.float32) * prec[date]
        weight_date[date] = here
        rhs_date[date] = here * obs[date]
    for date in range(dates_here):
        rhs[group * dates_here + date] = rhs_date[date, :, my_columns]
        weight[group * dates_here + date] = weight_date[date, :, my_columns]
    pl.semaphore_wait(barrier, greeted)

    def inward(field, source, target, step):
        peer = (group + step) % groups
        came_from = (group + groups - step) % groups
        block = source.at[:, :, pl.ds(pl.multiple_of(peer * width, width), width)]
        sent = pltpu.make_async_remote_copy(
            block, target.at[pl.ds(group * dates_here, dates_here)],
            send_sem.at[field, peer], recv_sem.at[field, group], (row, peer), MESH,
        )
        got = pltpu.make_async_remote_copy(
            block, target.at[pl.ds(came_from * dates_here, dates_here)],
            send_sem.at[field, peer], recv_sem.at[field, came_from], (row, peer), MESH,
        )
        return sent, got

    def outward(field, source, first, target, step):
        peer = (group + step) % groups
        came_from = (group + groups - step) % groups
        block = source.at[pl.ds(first + peer * dates_here, dates_here)]
        sent = pltpu.make_async_remote_copy(
            block, target.at[:, :, my_columns],
            send_sem.at[field, peer], recv_sem.at[field, group], (row, peer), MESH,
        )
        got = pltpu.make_async_remote_copy(
            block, target.at[:, :, pl.ds(pl.multiple_of(came_from * width, width), width)],
            send_sem.at[field, peer], recv_sem.at[field, came_from], (row, peer), MESH,
        )
        return sent, got

    half = groups // 2
    steps = sorted(range(1, groups), key=lambda step: (-min(step, groups - step), step))
    assert half >= 1
    rhs_copies = [inward(RHS, rhs_date, rhs, step) for step in steps]
    weight_copies = [inward(WEIGHT, weight_date, weight, step) for step in steps]
    for sent, _ in rhs_copies:
        sent.start()
    for sent, _ in weight_copies:
        sent.start()

    loads[3].wait()
    lane = lax.broadcasted_iota(jnp.int32, (height, LANES), 1)
    col = lax.broadcasted_iota(jnp.int32, (height, width), 1)
    line = lax.broadcasted_iota(jnp.int32, (height, width), 0)
    steps_across = 0.25 * (edge[0, :, my_columns].astype(jnp.float32) + 1.0)
    steps_down = 0.25 * (edge[1, :, my_columns].astype(jnp.float32) + 1.0)
    across[...] = jnp.where((col == width - 1) & (group == groups - 1), 0.0, steps_across)
    before = (left_group + 1) * width - LANES
    edge_before = edge[0, :, pl.ds(pl.multiple_of(before, LANES), LANES)].astype(jnp.float32)
    edge_before = pltpu.roll(0.25 * (edge_before + 1.0), 1, 1)
    edge_before = jnp.where(group == 0, 0.0, edge_before)

    def with_first(block, tile):
        first = jnp.where(lane == 0, tile, block[:, :LANES])
        if width == LANES:
            return first
        return jnp.concatenate([first, block[:, LANES:]], axis=1)

    def with_last(block, tile):
        last = jnp.where(lane == LANES - 1, tile, block[:, width - LANES :])
        if width == LANES:
            return last
        return jnp.concatenate([block[:, : width - LANES], last], axis=1)

    across_prev[...] = with_first(pltpu.roll(steps_across, 1, 1), edge_before)
    down_here = jnp.where((line == height - 1) & (row == rows - 1), 0.0, steps_down)
    downward[...] = down_here
    down_send[0, dates:, :] = jnp.broadcast_to(
        down_here[height - 1 :, :], (down_send.shape[1] - dates, width)
    )
    down_send[1, dates:, :] = jnp.zeros((down_send.shape[1] - dates, width), jnp.float32)
    for field in (precond, mapped):
        field[0] = jnp.zeros((height, width), jnp.float32)
        field[dates + 1] = jnp.zeros((height, width), jnp.float32)

    def folded(block):
        total = block[:, :LANES]
        for start in range(LANES, width, LANES):
            total = total + block[:, start : start + LANES]
        return total

    def over_dates(step_of, init):
        def several(index, carry):
            for inner in range(UNROLL):
                carry = step_of(index * UNROLL + inner, carry)
            return carry

        return lax.fori_loop(0, dates // UNROLL, several, init)

    none = jnp.zeros((height, LANES), jnp.float32)

    def precondition(source, target, turn):
        def one(date, carry):
            total, to_right, to_left = carry
            out = inv[date, 0].astype(jnp.float32) * source[0]
            for other in range(1, dates):
                out = out + inv[date, other].astype(jnp.float32) * source[other]
            target[date + 1] = out
            down_send[turn, pl.ds(date, 1), :] = out[height - 1 :, :]
            up_send[turn, pl.ds(date, 1), :] = out[:1, :]
            to_right = jnp.where(
                lane == date, pltpu.roll(out[:, width - LANES :], date + 1, 1), to_right
            )
            to_left = jnp.where(lane == date, pltpu.roll(out[:, :LANES], date, 1), to_left)
            return total + folded(source[date] * out), to_right, to_left

        total, to_right, to_left = over_dates(one, (none, none, none))
        right_send[turn] = to_right
        left_send[turn] = to_left
        return total

    def halo(turn):
        pairs = (
            (down_send, from_above, (below_row, group)),
            (up_send, from_below, (above_row, group)),
            (right_send, from_left, (row, right_group)),
            (left_send, from_right, (row, left_group)),
        )
        return [
            pltpu.make_async_remote_copy(
                source.at[turn], target.at[turn],
                halo_send_sem.at[turn, number], halo_recv_sem.at[turn, number], device, MESH,
            )
            for number, (source, target, device) in enumerate(pairs)
        ]

    def operator(field, target, turn):
        def one(date, total):
            here = field[date + 1]
            above = jnp.where(
                line == 0, from_above[turn, pl.ds(date, 1), :], pltpu.roll(here, 1, 0)
            )
            below = jnp.where(
                line == height - 1,
                from_below[turn, pl.ds(date, 1), :],
                pltpu.roll(here, height - 1, 0),
            )
            left = with_first(
                pltpu.roll(here, 1, 1),
                pltpu.roll(from_left[turn], (LANES - date) % LANES, 1),
            )
            right = with_last(
                pltpu.roll(here, width - 1, 1),
                pltpu.roll(from_right[turn], LANES - 1 - date, 1),
            )
            tau_up = jnp.where(date < dates - 1, tau_ref[jnp.minimum(date, dates - 2)], 0.0)
            tau_down = jnp.where(date > 0, tau_ref[jnp.maximum(date - 1, 0)], 0.0)
            out = (MASS + weight[date]) * here
            out = out + across[...] * (here - right) + across_prev[...] * (here - left)
            out = out + downward[...] * (here - below) + downward_prev[...] * (here - above)
            out = out + tau_up * (here - field[date + 2])
            out = out + tau_down * (here - field[date])
            target[date] = out
            return total + folded(here * out)

        return over_dates(one, none)

    def bring_back(field, source, first, target, chosen=steps):
        copies = [outward(field, source, first, target, step) for step in chosen]
        for sent, _ in copies:
            sent.start()
        if chosen[-1] != steps[-1]:
            return copies
        for date in range(dates_here):
            target[date, :, my_columns] = source[first + group * dates_here + date]
        return copies

    loads[4].wait()
    loads[5].wait()
    for _, got in rhs_copies:
        got.wait_recv()
    sum_rz = precondition(rhs, precond, 0)
    first_halo = halo(0)
    for copy in first_halo:
        copy.start()
    early = len(steps) // 3
    precond_copies = bring_back(PRECOND, precond, 1, precond_date, steps[:early])
    for _, got in weight_copies:
        got.wait_recv()
    for copy in first_halo:
        copy.wait_recv()
    downward_prev[...] = jnp.where(
        line == 0,
        jnp.where(row == 0, 0.0, from_above[0, dates : dates + 1, :]),
        pltpu.roll(downward[...], 1, 0),
    )
    sum_d = operator(precond, image, 0)
    sum_e = precondition(image, mapped, 1)
    second_halo = halo(1)
    for copy in second_halo:
        copy.start()
    precond_copies += bring_back(PRECOND, precond, 1, precond_date, steps[early:])
    for copy in second_halo:
        copy.wait_recv()
    sum_f = operator(mapped, second_image, 1)

    tile_line = lax.broadcasted_iota(jnp.int32, (height, LANES), 0)
    tile = jnp.zeros((height, LANES), jnp.float32)
    for number, total in enumerate((sum_rz, sum_d, sum_e, sum_f)):
        tile = jnp.where(tile_line == number, jnp.sum(total, axis=0, keepdims=True), tile)
    sum_copies = []
    for phase, (size, mine) in enumerate(phases):
        part[phase] = tile
        parts[phase, mine] = tile
        received = []
        for step in range(1, size):
            came_from = (mine + size - step) % size
            sent = pltpu.make_async_remote_copy(
                part.at[phase], parts.at[phase, mine],
                sum_send_sem.at[phase, step], sum_recv_sem.at[phase, mine],
                sum_peer(phase, step), MESH,
            )
            sent.start()
            sum_copies.append(sent)
            received.append(
                pltpu.make_async_remote_copy(
                    part.at[phase], parts.at[phase, came_from],
                    sum_send_sem.at[phase, step], sum_recv_sem.at[phase, came_from],
                    sum_peer(phase, step), MESH,
                )
            )
        if phase == 0:
            mapped_copies = bring_back(MAPPED, mapped, 1, mapped_date)
            image_copies = bring_back(IMAGE, image, 0, image_date)
            second_copies = bring_back(SECOND, second_image, 0, second_date)
        for got in received:
            got.wait_recv()
        tile = parts[phase, 0]
        for other in range(1, size):
            tile = tile + parts[phase, other]
    lines = jnp.sum(tile, axis=1, keepdims=True)
    rz, dd, ee, ff = (lines[number : number + 1] for number in range(4))
    alpha = rz / dd
    grown = alpha * ee / dd
    alpha_next = (alpha * alpha * ee - rz) / (alpha * alpha * (ff - ee * ee / dd))
    first = alpha + alpha_next * grown
    second = alpha_next * alpha
    first = jnp.broadcast_to(first, (height, width))
    second = jnp.broadcast_to(second, (height, width))

    def whole_row(output, combine, *copied):
        for copies in copied:
            for _, got in copies:
                got.wait_recv()
        for date in range(dates_here):
            for number in range(groups):
                output[date, :, number * width : (number + 1) * width] = combine(
                    (date, slice(None), slice(number * width, (number + 1) * width))
                )

    whole_row(
        sol_ref,
        lambda at: first * precond_date[at] - second * mapped_date[at],
        precond_copies, mapped_copies,
    )
    whole_row(
        res_ref,
        lambda at: rhs_date[at] - first * image_date[at] + second * second_date[at],
        image_copies, second_copies,
    )
    back = (precond_copies, image_copies, mapped_copies, second_copies)
    for copies in (rhs_copies, weight_copies) + back:
        for sent, _ in copies:
            sent.wait_send()
    for copy in first_halo + second_halo + sum_copies:
        copy.wait_send()


def body(obs_mask, precision, observed, edge_class, temporal_weight, inverse):
    rows, groups = lax.axis_size("rows"), lax.axis_size("dates")
    low_size = 8 if rows >= 64 else 2
    dates, _, height, width = inverse.shape
    f32 = jnp.float32
    whole = observed.shape
    block = (dates, height, width)
    padded = (dates + 2, height, width)
    most = max(groups, low_size, rows // low_size)
    vmem = pltpu.VMEM
    dma = pltpu.SemaphoreType.DMA
    scratch = (
        [vmem(whole, jnp.int32), vmem(whole, f32), vmem(whole, f32)]
        + [vmem(edge_class.shape, jnp.int32), vmem(inverse.shape, jnp.bfloat16)]
        + [vmem(whole, f32)] * 6
        + [vmem(block, f32), vmem(block, f32), vmem(padded, f32), vmem(block, f32)]
        + [vmem(padded, f32), vmem(block, f32)]
        + [vmem((height, width), f32)] * 4
        + [vmem((2, dates + 8, width), f32), vmem((2, dates, width), f32)] * 2
        + [vmem((2, height, LANES), f32)] * 4
        + [vmem((3, height, LANES), f32), vmem((3, most, height, LANES), f32)]
        + [pltpu.SMEM((dates - 1,), f32), dma((6,)), dma((6, groups)), dma((6, groups)), dma((2, 4)), dma((2, 4))]
        + [dma((3, most)), dma((3, most))]
    )
    anywhere = pl.BlockSpec(memory_space=pltpu.HBM)
    in_hbm = [
        pltpu.with_memory_space_constraint(array, pltpu.HBM)
        for array in (obs_mask, precision, observed, edge_class, temporal_weight, inverse)
    ]
    return pl.pallas_call(
        functools.partial(kernel, rows, groups, low_size),
        out_shape=[jax.ShapeDtypeStruct(whole, f32)] * 2,
        in_specs=[anywhere] * 6,
        out_specs=[pl.BlockSpec(memory_space=pltpu.VMEM)] * 2,
        scratch_shapes=scratch,
        compiler_params=pltpu.CompilerParams(collective_id=0, has_side_effects=True, vmem_limit_bytes=VMEM_BYTES),
        name="cg",
    )(*in_hbm)


def solution(mesh):
    return jax.shard_map(
        body,
        mesh=mesh,
        in_specs=(
            P("dates", "rows", None),
            P("dates", "rows", None),
            P("dates", "rows", None),
            P(None, "rows", None),
            P(),
            P(None, None, "rows", "dates"),
        ),
        out_specs=(P("dates", "rows", None), P("dates", "rows", None)),
        check_vma=False,
    )
```

```python
import functools
import jax
import jax.numpy as jnp
from jax import lax
from jax.experimental import pallas as pl
from jax.experimental.pallas import tpu as pltpu
from jax.sharding import PartitionSpec as P

MASS = 0.1
LANES = 128
UNROLL = 4
VMEM_BYTES = 16 * 1024 * 1024
MESH = pl.DeviceIdType.MESH
RHS, WEIGHT, PRECOND, MAPPED = range(4)


def kernel(
    rows, groups, low_size,
    mask_hbm, prec_hbm, obs_hbm, edge_hbm, tau_hbm, inv_hbm,
    sol_ref, res_ref,
    mask, prec, obs, edge, inv,
    weight_date, rhs_date, precond_date, mapped_date,
    weight, rhs, precond, image, mapped,
    date_down_send, date_up_send, from_above_date, from_below_date, from_before, from_after,
    across, across_prev, downward, downward_prev,
    down_send, up_send, from_above, from_below,
    right_send, left_send, from_left, from_right,
    part, parts,
    tau_ref, local_sem, send_sem, recv_sem, halo_send_sem, halo_recv_sem, date_send_sem, date_recv_sem, sum_send_sem, sum_recv_sem,
):
    dates_here, height, columns = mask.shape
    dates, _, width = rhs.shape
    row = lax.axis_index("rows")
    group = lax.axis_index("dates")
    low, high = row % low_size, row // low_size
    high_size = rows // low_size
    above_row, below_row = (row + rows - 1) % rows, (row + 1) % rows
    left_group, right_group = (group + groups - 1) % groups, (group + 1) % groups
    my_columns = pl.ds(pl.multiple_of(group * width, width), width)

    def sum_peer(phase, step):
        if phase == 0:
            return (row, (group + step) % groups)
        if phase == 1:
            return (high * low_size + (low + step) % low_size, group)
        return (((high + step) % high_size) * low_size + low, group)

    phases = ((groups, group), (low_size, low), (high_size, high))

    barrier = pltpu.get_barrier_semaphore()
    greeted = 0
    for phase, (size, _) in enumerate(phases):
        for step in range(1, size):
            pl.semaphore_signal(
                barrier, inc=1, device_id=sum_peer(phase, step), device_id_type=MESH
            )
            greeted += 1
    for neighbour in (above_row, below_row):
        pl.semaphore_signal(barrier, inc=1, device_id=(neighbour, group), device_id_type=MESH)
        greeted += 1

    loads = [
        pltpu.make_async_copy(source, target, local_sem.at[number])
        for number, (source, target) in enumerate(
            ((mask_hbm, mask), (prec_hbm, prec), (obs_hbm, obs), (edge_hbm, edge), (inv_hbm, inv), (tau_hbm, tau_ref))
        )
    ]
    for load in loads:
        load.start()

    for load in loads[:3]:
        load.wait()
    for date in range(dates_here):
        here = mask[date].astype(jnp.float32) * prec[date]
        weight_date[date] = here
        rhs_date[date] = here * obs[date]
    for date in range(dates_here):
        rhs[group * dates_here + date] = rhs_date[date, :, my_columns]
        weight[group * dates_here + date] = weight_date[date, :, my_columns]
    pl.semaphore_wait(barrier, greeted)

    def inward(field, source, target, step):
        peer = (group + step) % groups
        came_from = (group + groups - step) % groups
        block = source.at[:, :, pl.ds(pl.multiple_of(peer * width, width), width)]
        sent = pltpu.make_async_remote_copy(
            block, target.at[pl.ds(group * dates_here, dates_here)],
            send_sem.at[field, peer], recv_sem.at[field, group], (row, peer), MESH,
        )
        got = pltpu.make_async_remote_copy(
            block, target.at[pl.ds(came_from * dates_here, dates_here)],
            send_sem.at[field, peer], recv_sem.at[field, came_from], (row, peer), MESH,
        )
        return sent, got

    def outward(field, source, first, target, step):
        peer = (group + step) % groups
        came_from = (group + groups - step) % groups
        block = source.at[pl.ds(first + peer * dates_here, dates_here)]
        sent = pltpu.make_async_remote_copy(
            block, target.at[:, :, my_columns],
            send_sem.at[field, peer], recv_sem.at[field, group], (row, peer), MESH,
        )
        got = pltpu.make_async_remote_copy(
            block, target.at[:, :, pl.ds(pl.multiple_of(came_from * width, width), width)],
            send_sem.at[field, peer], recv_sem.at[field, came_from], (row, peer), MESH,
        )
        return sent, got

    half = groups // 2
    steps = sorted(range(1, groups), key=lambda step: (-min(step, groups - step), step))
    assert half >= 1
    rhs_copies = [inward(RHS, rhs_date, rhs, step) for step in steps]
    weight_copies = [inward(WEIGHT, weight_date, weight, step) for step in steps]
    for sent, _ in rhs_copies:
        sent.start()
    for sent, _ in weight_copies:
        sent.start()

    loads[3].wait()
    lane = lax.broadcasted_iota(jnp.int32, (height, LANES), 1)
    col = lax.broadcasted_iota(jnp.int32, (height, width), 1)
    line = lax.broadcasted_iota(jnp.int32, (height, width), 0)
    steps_across = 0.25 * (edge[0, :, my_columns].astype(jnp.float32) + 1.0)
    steps_down = 0.25 * (edge[1, :, my_columns].astype(jnp.float32) + 1.0)
    across[...] = jnp.where((col == width - 1) & (group == groups - 1), 0.0, steps_across)
    before = (left_group + 1) * width - LANES
    edge_before = edge[0, :, pl.ds(pl.multiple_of(before, LANES), LANES)].astype(jnp.float32)
    edge_before = pltpu.roll(0.25 * (edge_before + 1.0), 1, 1)
    edge_before = jnp.where(group == 0, 0.0, edge_before)

    def with_first(block, tile):
        first = jnp.where(lane == 0, tile, block[:, :LANES])
        if width == LANES:
            return first
        return jnp.concatenate([first, block[:, LANES:]], axis=1)

    def with_last(block, tile):
        last = jnp.where(lane == LANES - 1, tile, block[:, width - LANES :])
        if width == LANES:
            return last
        return jnp.concatenate([block[:, : width - LANES], last], axis=1)

    across_prev[...] = with_first(pltpu.roll(steps_across, 1, 1), edge_before)
    down_here = jnp.where((line == height - 1) & (row == rows - 1), 0.0, steps_down)
    downward[...] = down_here
    down_send[0, dates:, :] = jnp.broadcast_to(
        down_here[height - 1 :, :], (down_send.shape[1] - dates, width)
    )
    down_send[1, dates:, :] = jnp.zeros((down_send.shape[1] - dates, width), jnp.float32)
    rest = slice(dates_here, height)
    all_down = 0.25 * (edge[1, height - 1 :, :].astype(jnp.float32) + 1.0)
    for turn in range(2):
        date_down_send[turn, rest, :] = jnp.broadcast_to(all_down, (height - dates_here, columns))
        date_up_send[turn, rest, :] = jnp.zeros((height - dates_here, columns), jnp.float32)
    for field in (precond, mapped):
        field[0] = jnp.zeros((height, width), jnp.float32)
        field[dates + 1] = jnp.zeros((height, width), jnp.float32)

    def folded(block):
        total = block[:, :LANES]
        for start in range(LANES, width, LANES):
            total = total + block[:, start : start + LANES]
        return total

    def over_dates(step_of, init):
        def several(index, carry):
            for inner in range(UNROLL):
                carry = step_of(index * UNROLL + inner, carry)
            return carry

        return lax.fori_loop(0, dates // UNROLL, several, init)

    none = jnp.zeros((height, LANES), jnp.float32)

    def precondition(source, target, turn):
        def one(date, carry):
            total, to_right, to_left = carry
            out = inv[date, 0].astype(jnp.float32) * source[0]
            for other in range(1, dates):
                out = out + inv[date, other].astype(jnp.float32) * source[other]
            target[date + 1] = out
            down_send[turn, pl.ds(date, 1), :] = out[height - 1 :, :]
            up_send[turn, pl.ds(date, 1), :] = out[:1, :]
            to_right = jnp.where(
                lane == date, pltpu.roll(out[:, width - LANES :], date + 1, 1), to_right
            )
            to_left = jnp.where(lane == date, pltpu.roll(out[:, :LANES], date, 1), to_left)
            return total + folded(source[date] * out), to_right, to_left

        total, to_right, to_left = over_dates(one, (none, none, none))
        right_send[turn] = to_right
        left_send[turn] = to_left
        return total

    def halo(turn):
        pairs = (
            (down_send, from_above, (below_row, group)),
            (up_send, from_below, (above_row, group)),
            (right_send, from_left, (row, right_group)),
            (left_send, from_right, (row, left_group)),
        )
        return [
            pltpu.make_async_remote_copy(
                source.at[turn], target.at[turn],
                halo_send_sem.at[turn, number], halo_recv_sem.at[turn, number], device, MESH,
            )
            for number, (source, target, device) in enumerate(pairs)
        ]

    def operator(field, target, turn):
        def one(date, total):
            here = field[date + 1]
            above = jnp.where(
                line == 0, from_above[turn, pl.ds(date, 1), :], pltpu.roll(here, 1, 0)
            )
            below = jnp.where(
                line == height - 1,
                from_below[turn, pl.ds(date, 1), :],
                pltpu.roll(here, height - 1, 0),
            )
            left = with_first(
                pltpu.roll(here, 1, 1),
                pltpu.roll(from_left[turn], (LANES - date) % LANES, 1),
            )
            right = with_last(
                pltpu.roll(here, width - 1, 1),
                pltpu.roll(from_right[turn], LANES - 1 - date, 1),
            )
            tau_up = jnp.where(date < dates - 1, tau_ref[jnp.minimum(date, dates - 2)], 0.0)
            tau_down = jnp.where(date > 0, tau_ref[jnp.maximum(date - 1, 0)], 0.0)
            out = (MASS + weight[date]) * here
            out = out + across[...] * (here - right) + across_prev[...] * (here - left)
            out = out + downward[...] * (here - below) + downward_prev[...] * (here - above)
            out = out + tau_up * (here - field[date + 2])
            out = out + tau_down * (here - field[date])
            if target is not None:
                target[date] = out
            return total + folded(here * out)

        return over_dates(one, none)

    def bring_back(field, source, first, target, chosen=steps):
        copies = [outward(field, source, first, target, step) for step in chosen]
        for sent, _ in copies:
            sent.start()
        if chosen[-1] != steps[-1]:
            return copies
        for date in range(dates_here):
            target[date, :, my_columns] = source[first + group * dates_here + date]
        return copies

    loads[4].wait()
    loads[5].wait()
    for _, got in rhs_copies:
        got.wait_recv()
    sum_rz = precondition(rhs, precond, 0)
    first_halo = halo(0)
    for copy in first_halo:
        copy.start()
    early = len(steps) // 3
    precond_copies = bring_back(PRECOND, precond, 1, precond_date, steps[:early])
    for _, got in weight_copies:
        got.wait_recv()
    for copy in first_halo:
        copy.wait_recv()
    downward_prev[...] = jnp.where(
        line == 0,
        jnp.where(row == 0, 0.0, from_above[0, dates : dates + 1, :]),
        pltpu.roll(downward[...], 1, 0),
    )
    sum_d = operator(precond, image, 0)
    sum_e = precondition(image, mapped, 1)
    second_halo = halo(1)
    for copy in second_halo:
        copy.start()
    precond_copies += bring_back(PRECOND, precond, 1, precond_date, steps[early:])
    for copy in second_halo:
        copy.wait_recv()
    sum_f = operator(mapped, None, 1)

    def date_halo(turn, field, copies):
        for _, got in copies:
            got.wait_recv()
        for date in range(dates_here):
            date_down_send[turn, date : date + 1, :] = field[date, height - 1 :, :]
            date_up_send[turn, date : date + 1, :] = field[date, :1, :]
        pairs = (
            (date_down_send.at[turn], from_above_date, (below_row, group)),
            (date_up_send.at[turn], from_below_date, (above_row, group)),
            (field.at[dates_here - 1], from_before, (row, right_group)),
            (field.at[0], from_after, (row, left_group)),
        )
        started = [
            pltpu.make_async_remote_copy(
                source, target.at[turn],
                date_send_sem.at[turn, number], date_recv_sem.at[turn, number], device, MESH,
            )
            for number, (source, target, device) in enumerate(pairs)
        ]
        for copy in started:
            copy.start()
        return started

    tile_line = lax.broadcasted_iota(jnp.int32, (height, LANES), 0)
    tile = jnp.zeros((height, LANES), jnp.float32)
    for number, total in enumerate((sum_rz, sum_d, sum_e, sum_f)):
        tile = jnp.where(tile_line == number, jnp.sum(total, axis=0, keepdims=True), tile)
    sum_copies = []
    for phase, (size, mine) in enumerate(phases):
        part[phase] = tile
        parts[phase, mine] = tile
        received = []
        for step in range(1, size):
            came_from = (mine + size - step) % size
            sent = pltpu.make_async_remote_copy(
                part.at[phase], parts.at[phase, mine],
                sum_send_sem.at[phase, step], sum_recv_sem.at[phase, mine],
                sum_peer(phase, step), MESH,
            )
            sent.start()
            sum_copies.append(sent)
            received.append(
                pltpu.make_async_remote_copy(
                    part.at[phase], parts.at[phase, came_from],
                    sum_send_sem.at[phase, step], sum_recv_sem.at[phase, came_from],
                    sum_peer(phase, step), MESH,
                )
            )
        if phase == 0:
            mapped_copies = bring_back(MAPPED, mapped, 1, mapped_date)
            precond_halo = date_halo(0, precond_date, precond_copies)
        if phase == 2:
            mapped_halo = date_halo(1, mapped_date, mapped_copies)
        for got in received:
            got.wait_recv()
        tile = parts[phase, 0]
        for other in range(1, size):
            tile = tile + parts[phase, other]
    lines = jnp.sum(tile, axis=1, keepdims=True)
    rz, dd, ee, ff = (lines[number : number + 1] for number in range(4))
    alpha = rz / dd
    grown = alpha * ee / dd
    alpha_next = (alpha * alpha * ee - rz) / (alpha * alpha * (ff - ee * ee / dd))
    first = alpha + alpha_next * grown
    second = alpha_next * alpha
    first = jnp.broadcast_to(first, (height, width))
    second = jnp.broadcast_to(second, (height, width))

    def combined(at_precond, at_mapped):
        return first * at_precond - second * at_mapped

    spans = [slice(number * width, (number + 1) * width) for number in range(groups)]
    for date in range(dates_here):
        for span in spans:
            sol_ref[date, :, span] = combined(
                precond_date[date, :, span], mapped_date[date, :, span]
            )
    for copy in precond_halo + mapped_halo:
        copy.wait_recv()

    for number, span in enumerate(spans):
        tile_before = slice(max(span.start - LANES, 0), max(span.start, LANES))
        tile_after = slice(min(span.stop, columns - LANES), min(span.stop + LANES, columns))
        ahead = 0.25 * (edge[0, :, span].astype(jnp.float32) + 1.0)
        behind = 0.25 * (edge[0, :, tile_before].astype(jnp.float32) + 1.0)
        behind = with_first(pltpu.roll(ahead, 1, 1), pltpu.roll(behind, 1, 1))
        if number == 0:
            behind = jnp.where(col == 0, 0.0, behind)
        if number == groups - 1:
            ahead = jnp.where(col == width - 1, 0.0, ahead)
        under = 0.25 * (edge[1, :, span].astype(jnp.float32) + 1.0)
        under = jnp.where((line == height - 1) & (row == rows - 1), 0.0, under)
        over = jnp.where(
            line == 0,
            jnp.where(row == 0, 0.0, from_above_date[0, dates_here : dates_here + 1, span]),
            pltpu.roll(under, 1, 0),
        )
        for date in range(dates_here):
            when = group * dates_here + date
            tau_up = jnp.where(when < dates - 1, tau_ref[jnp.minimum(when, dates - 2)], 0.0)
            tau_down = jnp.where(when > 0, tau_ref[jnp.maximum(when - 1, 0)], 0.0)
            here = sol_ref[date, :, span]
            this = slice(date, date + 1)
            above = combined(from_above_date[0, this, span], from_above_date[1, this, span])
            below = combined(from_below_date[0, this, span], from_below_date[1, this, span])
            above = jnp.where(line == 0, above, pltpu.roll(here, 1, 0))
            below = jnp.where(line == height - 1, below, pltpu.roll(here, height - 1, 0))
            left = with_first(
                pltpu.roll(here, 1, 1), pltpu.roll(sol_ref[date, :, tile_before], 1, 1)
            )
            right = with_last(
                pltpu.roll(here, width - 1, 1),
                pltpu.roll(sol_ref[date, :, tile_after], LANES - 1, 1),
            )
            if date > 0:
                before_here = sol_ref[date - 1, :, span]
            else:
                before_here = combined(from_before[0, :, span], from_before[1, :, span])
            if date + 1 < dates_here:
                after_here = sol_ref[date + 1, :, span]
            else:
                after_here = combined(from_after[0, :, span], from_after[1, :, span])
            out = (MASS + weight_date[date, :, span]) * here
            out = out + ahead * (here - right) + behind * (here - left)
            out = out + under * (here - below) + over * (here - above)
            out = out + tau_up * (here - after_here) + tau_down * (here - before_here)
            res_ref[date, :, span] = rhs_date[date, :, span] - out
    back = (precond_copies, mapped_copies)
    for copies in (rhs_copies, weight_copies) + back:
        for sent, _ in copies:
            sent.wait_send()
    for copy in first_halo + second_halo + precond_halo + mapped_halo + sum_copies:
        copy.wait_send()


def body(obs_mask, precision, observed, edge_class, temporal_weight, inverse):
    rows, groups = lax.axis_size("rows"), lax.axis_size("dates")
    low_size = 8 if rows >= 64 else 2
    dates, _, height, width = inverse.shape
    f32 = jnp.float32
    whole = observed.shape
    block = (dates, height, width)
    padded = (dates + 2, height, width)
    most = max(groups, low_size, rows // low_size)
    vmem = pltpu.VMEM
    dma = pltpu.SemaphoreType.DMA
    scratch = (
        [vmem(whole, jnp.int32), vmem(whole, f32), vmem(whole, f32)]
        + [vmem(edge_class.shape, jnp.int32), vmem(inverse.shape, jnp.bfloat16)]
        + [vmem(whole, f32)] * 4
        + [vmem(block, f32), vmem(block, f32), vmem(padded, f32), vmem(block, f32)]
        + [vmem(padded, f32)]
        + [vmem((2, height, whole[2]), f32)] * 6
        + [vmem((height, width), f32)] * 4
        + [vmem((2, dates + 8, width), f32), vmem((2, dates, width), f32)] * 2
        + [vmem((2, height, LANES), f32)] * 4
        + [vmem((3, height, LANES), f32), vmem((3, most, height, LANES), f32)]
        + [pltpu.SMEM((dates - 1,), f32), dma((6,)), dma((4, groups)), dma((4, groups))] + [dma((2, 4))] * 4
        + [dma((3, most)), dma((3, most))]
    )
    anywhere = pl.BlockSpec(memory_space=pltpu.HBM)
    in_hbm = [
        pltpu.with_memory_space_constraint(array, pltpu.HBM)
        for array in (obs_mask, precision, observed, edge_class, temporal_weight, inverse)
    ]
    return pl.pallas_call(
        functools.partial(kernel, rows, groups, low_size),
        out_shape=[jax.ShapeDtypeStruct(whole, f32)] * 2,
        in_specs=[anywhere] * 6,
        out_specs=[pl.BlockSpec(memory_space=pltpu.VMEM)] * 2,
        scratch_shapes=scratch,
        compiler_params=pltpu.CompilerParams(collective_id=0, has_side_effects=True, vmem_limit_bytes=VMEM_BYTES),
        name="cg",
    )(*in_hbm)


def solution(mesh):
    return jax.shard_map(
        body,
        mesh=mesh,
        in_specs=(
            P("dates", "rows", None),
            P("dates", "rows", None),
            P("dates", "rows", None),
            P(None, "rows", None),
            P(),
            P(None, None, "rows", "dates"),
        ),
        out_specs=(P("dates", "rows", None), P("dates", "rows", None)),
        check_vma=False,
    )
```

```python
import functools
import jax
import jax.numpy as jnp
from jax import lax
from jax.experimental import pallas as pl
from jax.experimental.pallas import tpu as pltpu
from jax.sharding import PartitionSpec as P

MASS = 0.1
LANES = 128
UNROLL = 4
VMEM_BYTES = 16 * 1024 * 1024
MESH = pl.DeviceIdType.MESH
RHS, WEIGHT, PRECOND, MAPPED = range(4)


def kernel(
    rows, groups, low_size,
    mask_hbm, prec_hbm, obs_hbm, edge_hbm, tau_hbm, inv_hbm,
    sol_ref, res_ref,
    mask, prec, obs, edge, inv,
    weight_date, rhs_date, precond_date, mapped_date,
    weight, rhs, precond, image, mapped,
    date_down_send, date_up_send, from_above_date, from_below_date, from_before, from_after,
    across, across_prev, downward, downward_prev,
    down_send, up_send, from_above, from_below,
    right_send, left_send, from_left, from_right,
    part, parts,
    tau_ref, local_sem, send_sem, recv_sem, halo_send_sem, halo_recv_sem, date_send_sem, date_recv_sem, sum_send_sem, sum_recv_sem,
):
    dates_here, height, columns = mask.shape
    dates, _, width = rhs.shape
    row = lax.axis_index("rows")
    group = lax.axis_index("dates")
    low, high = row % low_size, row // low_size
    high_size = rows // low_size
    above_row, below_row = (row + rows - 1) % rows, (row + 1) % rows
    left_group, right_group = (group + groups - 1) % groups, (group + 1) % groups
    my_columns = pl.ds(pl.multiple_of(group * width, width), width)

    def sum_peer(phase, step):
        if phase == 0:
            return (row, (group + step) % groups)
        if phase == 1:
            return (high * low_size + (low + step) % low_size, group)
        return (((high + step) % high_size) * low_size + low, group)

    phases = ((groups, group), (low_size, low), (high_size, high))

    barrier = pltpu.get_barrier_semaphore()
    greeted = 0
    for phase, (size, _) in enumerate(phases):
        for step in range(1, size):
            pl.semaphore_signal(
                barrier, inc=1, device_id=sum_peer(phase, step), device_id_type=MESH
            )
            greeted += 1
    for neighbour in (above_row, below_row):
        pl.semaphore_signal(barrier, inc=1, device_id=(neighbour, group), device_id_type=MESH)
        greeted += 1

    loads = [
        pltpu.make_async_copy(source, target, local_sem.at[number])
        for number, (source, target) in enumerate(
            ((mask_hbm, mask), (prec_hbm, prec), (obs_hbm, obs), (edge_hbm, edge), (inv_hbm, inv), (tau_hbm, tau_ref))
        )
    ]
    for load in loads:
        load.start()

    for load in loads[:3]:
        load.wait()
    for date in range(dates_here):
        here = mask[date].astype(jnp.float32) * prec[date]
        weight_date[date] = here
        rhs_date[date] = here * obs[date]
    for date in range(dates_here):
        rhs[group * dates_here + date] = rhs_date[date, :, my_columns]
        weight[group * dates_here + date] = weight_date[date, :, my_columns]
    pl.semaphore_wait(barrier, greeted)

    def inward(field, source, target, step):
        peer = (group + step) % groups
        came_from = (group + groups - step) % groups
        block = source.at[:, :, pl.ds(pl.multiple_of(peer * width, width), width)]
        sent = pltpu.make_async_remote_copy(
            block, target.at[pl.ds(group * dates_here, dates_here)],
            send_sem.at[field, peer], recv_sem.at[field, group], (row, peer), MESH,
        )
        got = pltpu.make_async_remote_copy(
            block, target.at[pl.ds(came_from * dates_here, dates_here)],
            send_sem.at[field, peer], recv_sem.at[field, came_from], (row, peer), MESH,
        )
        return sent, got

    def outward(field, source, first, target, step):
        peer = (group + step) % groups
        came_from = (group + groups - step) % groups
        block = source.at[pl.ds(first + peer * dates_here, dates_here)]
        sent = pltpu.make_async_remote_copy(
            block, target.at[:, :, my_columns],
            send_sem.at[field, peer], recv_sem.at[field, group], (row, peer), MESH,
        )
        got = pltpu.make_async_remote_copy(
            block, target.at[:, :, pl.ds(pl.multiple_of(came_from * width, width), width)],
            send_sem.at[field, peer], recv_sem.at[field, came_from], (row, peer), MESH,
        )
        return sent, got

    half = groups // 2
    steps = sorted(range(1, groups), key=lambda step: (-min(step, groups - step), step))
    assert half >= 1
    rhs_copies = [inward(RHS, rhs_date, rhs, step) for step in steps]
    weight_copies = [inward(WEIGHT, weight_date, weight, step) for step in steps]
    for sent, _ in rhs_copies:
        sent.start()
    for sent, _ in weight_copies:
        sent.start()

    loads[3].wait()
    lane = lax.broadcasted_iota(jnp.int32, (height, LANES), 1)
    col = lax.broadcasted_iota(jnp.int32, (height, width), 1)
    line = lax.broadcasted_iota(jnp.int32, (height, width), 0)
    steps_across = 0.25 * (edge[0, :, my_columns].astype(jnp.float32) + 1.0)
    steps_down = 0.25 * (edge[1, :, my_columns].astype(jnp.float32) + 1.0)
    across[...] = jnp.where((col == width - 1) & (group == groups - 1), 0.0, steps_across)
    before = (left_group + 1) * width - LANES
    edge_before = edge[0, :, pl.ds(pl.multiple_of(before, LANES), LANES)].astype(jnp.float32)
    edge_before = pltpu.roll(0.25 * (edge_before + 1.0), 1, 1)
    edge_before = jnp.where(group == 0, 0.0, edge_before)

    def with_first(block, tile):
        first = jnp.where(lane == 0, tile, block[:, :LANES])
        if width == LANES:
            return first
        return jnp.concatenate([first, block[:, LANES:]], axis=1)

    def with_last(block, tile):
        last = jnp.where(lane == LANES - 1, tile, block[:, width - LANES :])
        if width == LANES:
            return last
        return jnp.concatenate([block[:, : width - LANES], last], axis=1)

    across_prev[...] = with_first(pltpu.roll(steps_across, 1, 1), edge_before)
    down_here = jnp.where((line == height - 1) & (row == rows - 1), 0.0, steps_down)
    downward[...] = down_here
    down_send[0, dates:, :] = jnp.broadcast_to(
        down_here[height - 1 :, :], (down_send.shape[1] - dates, width)
    )
    down_send[1, dates:, :] = jnp.zeros((down_send.shape[1] - dates, width), jnp.float32)
    rest = slice(dates_here, height)
    all_down = 0.25 * (edge[1, height - 1 :, :].astype(jnp.float32) + 1.0)
    for turn in range(2):
        date_down_send[turn, rest, :] = jnp.broadcast_to(all_down, (height - dates_here, columns))
        date_up_send[turn, rest, :] = jnp.zeros((height - dates_here, columns), jnp.float32)
    for field in (precond, mapped):
        field[0] = jnp.zeros((height, width), jnp.float32)
        field[dates + 1] = jnp.zeros((height, width), jnp.float32)

    def folded(block):
        total = block[:, :LANES]
        for start in range(LANES, width, LANES):
            total = total + block[:, start : start + LANES]
        return total

    def over_dates(step_of, init):
        def several(index, carry):
            for inner in range(UNROLL):
                carry = step_of(index * UNROLL + inner, carry)
            return carry

        return lax.fori_loop(0, dates // UNROLL, several, init)

    none = jnp.zeros((height, LANES), jnp.float32)

    def precondition(source, target, turn):
        def one(date, carry):
            total, to_right, to_left = carry
            out = inv[date, 0].astype(jnp.float32) * source[0]
            for other in range(1, dates):
                out = out + inv[date, other].astype(jnp.float32) * source[other]
            target[date + 1] = out
            down_send[turn, pl.ds(date, 1), :] = out[height - 1 :, :]
            up_send[turn, pl.ds(date, 1), :] = out[:1, :]
            to_right = jnp.where(
                lane == date, pltpu.roll(out[:, width - LANES :], date + 1, 1), to_right
            )
            to_left = jnp.where(lane == date, pltpu.roll(out[:, :LANES], date, 1), to_left)
            return total + folded(source[date] * out), to_right, to_left

        total, to_right, to_left = over_dates(one, (none, none, none))
        right_send[turn] = to_right
        left_send[turn] = to_left
        return total

    def halo(turn):
        pairs = (
            (down_send, from_above, (below_row, group)),
            (up_send, from_below, (above_row, group)),
            (right_send, from_left, (row, right_group)),
            (left_send, from_right, (row, left_group)),
        )
        return [
            pltpu.make_async_remote_copy(
                source.at[turn], target.at[turn],
                halo_send_sem.at[turn, number], halo_recv_sem.at[turn, number], device, MESH,
            )
            for number, (source, target, device) in enumerate(pairs)
        ]

    def operator(field, target, turn):
        def one(date, total):
            here = field[date + 1]
            above = jnp.where(
                line == 0, from_above[turn, pl.ds(date, 1), :], pltpu.roll(here, 1, 0)
            )
            below = jnp.where(
                line == height - 1,
                from_below[turn, pl.ds(date, 1), :],
                pltpu.roll(here, height - 1, 0),
            )
            left = with_first(
                pltpu.roll(here, 1, 1),
                pltpu.roll(from_left[turn], (LANES - date) % LANES, 1),
            )
            right = with_last(
                pltpu.roll(here, width - 1, 1),
                pltpu.roll(from_right[turn], LANES - 1 - date, 1),
            )
            tau_up = jnp.where(date < dates - 1, tau_ref[jnp.minimum(date, dates - 2)], 0.0)
            tau_down = jnp.where(date > 0, tau_ref[jnp.maximum(date - 1, 0)], 0.0)
            out = (MASS + weight[date]) * here
            out = out + across[...] * (here - right) + across_prev[...] * (here - left)
            out = out + downward[...] * (here - below) + downward_prev[...] * (here - above)
            out = out + tau_up * (here - field[date + 2])
            out = out + tau_down * (here - field[date])
            if target is not None:
                target[date] = out
            return total + folded(here * out)

        return over_dates(one, none)

    def bring_back(field, source, first, target, chosen=steps):
        copies = [outward(field, source, first, target, step) for step in chosen]
        for sent, _ in copies:
            sent.start()
        if chosen[-1] != steps[-1]:
            return copies
        for date in range(dates_here):
            target[date, :, my_columns] = source[first + group * dates_here + date]
        return copies

    loads[4].wait()
    loads[5].wait()
    for _, got in rhs_copies:
        got.wait_recv()
    sum_rz = precondition(rhs, precond, 0)
    first_halo = halo(0)
    for copy in first_halo:
        copy.start()
    early = len(steps) // 3
    precond_copies = bring_back(PRECOND, precond, 1, precond_date, steps[:early])
    for _, got in weight_copies:
        got.wait_recv()
    for copy in first_halo:
        copy.wait_recv()
    downward_prev[...] = jnp.where(
        line == 0,
        jnp.where(row == 0, 0.0, from_above[0, dates : dates + 1, :]),
        pltpu.roll(downward[...], 1, 0),
    )
    sum_d = operator(precond, image, 0)
    sum_e = precondition(image, mapped, 1)
    second_halo = halo(1)
    for copy in second_halo:
        copy.start()
    precond_copies += bring_back(PRECOND, precond, 1, precond_date, steps[early:])
    for copy in second_halo:
        copy.wait_recv()
    sum_f = operator(mapped, None, 1)

    def date_halo(turn, field, copies):
        for _, got in copies:
            got.wait_recv()
        for date in range(dates_here):
            date_down_send[turn, date : date + 1, :] = field[date, height - 1 :, :]
            date_up_send[turn, date : date + 1, :] = field[date, :1, :]
        pairs = (
            (date_down_send.at[turn], from_above_date, (below_row, group)),
            (date_up_send.at[turn], from_below_date, (above_row, group)),
            (field.at[dates_here - 1], from_before, (row, right_group)),
            (field.at[0], from_after, (row, left_group)),
        )
        started = [
            pltpu.make_async_remote_copy(
                source, target.at[turn],
                date_send_sem.at[turn, number], date_recv_sem.at[turn, number], device, MESH,
            )
            for number, (source, target, device) in enumerate(pairs)
        ]
        for copy in started:
            copy.start()
        return started

    tile_line = lax.broadcasted_iota(jnp.int32, (height, LANES), 0)
    tile = jnp.zeros((height, LANES), jnp.float32)
    for number, total in enumerate((sum_rz, sum_d, sum_e, sum_f)):
        tile = jnp.where(tile_line == number, jnp.sum(total, axis=0, keepdims=True), tile)
    sum_copies = []
    for phase, (size, mine) in enumerate(phases):
        part[phase] = tile
        parts[phase, mine] = tile
        received = []
        for step in range(1, size):
            came_from = (mine + size - step) % size
            sent = pltpu.make_async_remote_copy(
                part.at[phase], parts.at[phase, mine],
                sum_send_sem.at[phase, step], sum_recv_sem.at[phase, mine],
                sum_peer(phase, step), MESH,
            )
            sent.start()
            sum_copies.append(sent)
            received.append(
                pltpu.make_async_remote_copy(
                    part.at[phase], parts.at[phase, came_from],
                    sum_send_sem.at[phase, step], sum_recv_sem.at[phase, came_from],
                    sum_peer(phase, step), MESH,
                )
            )
        if phase == 0:
            mapped_copies = bring_back(MAPPED, mapped, 1, mapped_date)
            precond_halo = date_halo(0, precond_date, precond_copies)
        if phase == 2:
            mapped_halo = date_halo(1, mapped_date, mapped_copies)
        for got in received:
            got.wait_recv()
        tile = parts[phase, 0]
        for other in range(1, size):
            tile = tile + parts[phase, other]
    lines = jnp.sum(tile, axis=1, keepdims=True)
    rz, dd, ee, ff = (lines[number : number + 1] for number in range(4))
    alpha = rz / dd
    grown = alpha * ee / dd
    alpha_next = (alpha * alpha * ee - rz) / (alpha * alpha * (ff - ee * ee / dd))
    first = alpha + alpha_next * grown
    second = alpha_next * alpha
    first = jnp.broadcast_to(first, (height, width))
    second = jnp.broadcast_to(second, (height, width))

    def combined(at_precond, at_mapped):
        return first * at_precond - second * at_mapped

    spans = [slice(number * width, (number + 1) * width) for number in range(groups)]
    for date in range(dates_here):
        for span in spans:
            sol_ref[date, :, span] = combined(
                precond_date[date, :, span], mapped_date[date, :, span]
            )
    for copy in precond_halo[:2] + mapped_halo[:2]:
        copy.wait_recv()

    between = []
    for date in range(dates_here + 1):
        when = group * dates_here + date
        inside = (when > 0) & (when < dates)
        place = jnp.minimum(jnp.maximum(when - 1, 0), dates - 2)
        between.append(jnp.where(inside, tau_ref[place], 0.0))

    for number, span in enumerate(spans):
        tile_before = slice(max(span.start - LANES, 0), max(span.start, LANES))
        tile_after = slice(min(span.stop, columns - LANES), min(span.stop + LANES, columns))
        ahead = 0.25 * (edge[0, :, span].astype(jnp.float32) + 1.0)
        behind = 0.25 * (edge[0, :, tile_before].astype(jnp.float32) + 1.0)
        behind = with_first(pltpu.roll(ahead, 1, 1), pltpu.roll(behind, 1, 1))
        if number == 0:
            behind = jnp.where(col == 0, 0.0, behind)
        if number == groups - 1:
            ahead = jnp.where(col == width - 1, 0.0, ahead)
        under = 0.25 * (edge[1, :, span].astype(jnp.float32) + 1.0)
        under = jnp.where((line == height - 1) & (row == rows - 1), 0.0, under)
        over = jnp.where(
            line == 0,
            jnp.where(row == 0, 0.0, from_above_date[0, dates_here : dates_here + 1, span]),
            pltpu.roll(under, 1, 0),
        )
        for date in range(dates_here):
            here = sol_ref[date, :, span]
            this = slice(date, date + 1)
            above = combined(from_above_date[0, this, span], from_above_date[1, this, span])
            below = combined(from_below_date[0, this, span], from_below_date[1, this, span])
            above = jnp.where(line == 0, above, pltpu.roll(here, 1, 0))
            below = jnp.where(line == height - 1, below, pltpu.roll(here, height - 1, 0))
            left = with_first(
                pltpu.roll(here, 1, 1), pltpu.roll(sol_ref[date, :, tile_before], 1, 1)
            )
            right = with_last(
                pltpu.roll(here, width - 1, 1),
                pltpu.roll(sol_ref[date, :, tile_after], LANES - 1, 1),
            )
            out = (MASS + weight_date[date, :, span]) * here
            out = out + ahead * (here - right) + behind * (here - left)
            out = out + under * (here - below) + over * (here - above)
            if date > 0:
                out = out + between[date] * (here - sol_ref[date - 1, :, span])
            if date + 1 < dates_here:
                out = out + between[date + 1] * (here - sol_ref[date + 1, :, span])
            res_ref[date, :, span] = rhs_date[date, :, span] - out
    for copy in precond_halo[2:] + mapped_halo[2:]:
        copy.wait_recv()
    for span in spans:
        for date, weight_out, other in (
            (0, between[0], from_before),
            (dates_here - 1, between[dates_here], from_after),
        ):
            there = combined(other[0, :, span], other[1, :, span])
            res_ref[date, :, span] = res_ref[date, :, span] - weight_out * (
                sol_ref[date, :, span] - there
            )
    back = (precond_copies, mapped_copies)
    for copies in (rhs_copies, weight_copies) + back:
        for sent, _ in copies:
            sent.wait_send()
    for copy in first_halo + second_halo + precond_halo + mapped_halo + sum_copies:
        copy.wait_send()


def body(obs_mask, precision, observed, edge_class, temporal_weight, inverse):
    rows, groups = lax.axis_size("rows"), lax.axis_size("dates")
    low_size = 8 if rows >= 64 else 2
    dates, _, height, width = inverse.shape
    f32 = jnp.float32
    whole = observed.shape
    block = (dates, height, width)
    padded = (dates + 2, height, width)
    most = max(groups, low_size, rows // low_size)
    vmem = pltpu.VMEM
    dma = pltpu.SemaphoreType.DMA
    scratch = (
        [vmem(whole, jnp.int32), vmem(whole, f32), vmem(whole, f32)]
        + [vmem(edge_class.shape, jnp.int32), vmem(inverse.shape, jnp.bfloat16)]
        + [vmem(whole, f32)] * 4
        + [vmem(block, f32), vmem(block, f32), vmem(padded, f32), vmem(block, f32)]
        + [vmem(padded, f32)]
        + [vmem((2, height, whole[2]), f32)] * 6
        + [vmem((height, width), f32)] * 4
        + [vmem((2, dates + 8, width), f32), vmem((2, dates, width), f32)] * 2
        + [vmem((2, height, LANES), f32)] * 4
        + [vmem((3, height, LANES), f32), vmem((3, most, height, LANES), f32)]
        + [pltpu.SMEM((dates - 1,), f32), dma((6,)), dma((4, groups)), dma((4, groups))] + [dma((2, 4))] * 4
        + [dma((3, most)), dma((3, most))]
    )
    anywhere = pl.BlockSpec(memory_space=pltpu.HBM)
    in_hbm = [
        pltpu.with_memory_space_constraint(array, pltpu.HBM)
        for array in (obs_mask, precision, observed, edge_class, temporal_weight, inverse)
    ]
    return pl.pallas_call(
        functools.partial(kernel, rows, groups, low_size),
        out_shape=[jax.ShapeDtypeStruct(whole, f32)] * 2,
        in_specs=[anywhere] * 6,
        out_specs=[pl.BlockSpec(memory_space=pltpu.VMEM)] * 2,
        scratch_shapes=scratch,
        compiler_params=pltpu.CompilerParams(collective_id=0, has_side_effects=True, vmem_limit_bytes=VMEM_BYTES),
        name="cg",
    )(*in_hbm)


def solution(mesh):
    return jax.shard_map(
        body,
        mesh=mesh,
        in_specs=(
            P("dates", "rows", None),
            P("dates", "rows", None),
            P("dates", "rows", None),
            P(None, "rows", None),
            P(),
            P(None, None, "rows", "dates"),
        ),
        out_specs=(P("dates", "rows", None), P("dates", "rows", None)),
        check_vma=False,
    )
```

```python
import functools
import jax
import jax.numpy as jnp
from jax import lax
from jax.experimental import pallas as pl
from jax.experimental.pallas import tpu as pltpu
from jax.sharding import PartitionSpec as P

MASS = 0.1
LANES = 128
UNROLL = 8
VMEM_BYTES = 16 * 1024 * 1024
MESH = pl.DeviceIdType.MESH
RHS, WEIGHT, PRECOND, MAPPED = range(4)


def kernel(
    rows, groups, low_size,
    mask_hbm, prec_hbm, obs_hbm, edge_hbm, tau_hbm, inv_hbm,
    sol_ref, res_ref,
    mask, prec, obs, edge, inv,
    weight_date, rhs_date, precond_date, mapped_date,
    weight, rhs, precond, image, mapped,
    date_down_send, date_up_send, from_above_date, from_below_date, from_before, from_after,
    across, across_prev, downward, downward_prev,
    down_send, up_send, from_above, from_below,
    right_send, left_send, from_left, from_right,
    part, parts,
    tau_ref, local_sem, send_sem, recv_sem, halo_send_sem, halo_recv_sem, date_send_sem, date_recv_sem, sum_send_sem, sum_recv_sem,
):
    dates_here, height, columns = mask.shape
    dates, _, width = rhs.shape
    row = lax.axis_index("rows")
    group = lax.axis_index("dates")
    low, high = row % low_size, row // low_size
    high_size = rows // low_size
    above_row, below_row = (row + rows - 1) % rows, (row + 1) % rows
    left_group, right_group = (group + groups - 1) % groups, (group + 1) % groups
    my_columns = pl.ds(pl.multiple_of(group * width, width), width)

    def sum_peer(phase, step):
        if phase == 0:
            return (row, (group + step) % groups)
        if phase == 1:
            return (high * low_size + (low + step) % low_size, group)
        return (((high + step) % high_size) * low_size + low, group)

    phases = ((groups, group), (low_size, low), (high_size, high))

    barrier = pltpu.get_barrier_semaphore()
    greeted = 0
    for phase, (size, _) in enumerate(phases):
        for step in range(1, size):
            pl.semaphore_signal(
                barrier, inc=1, device_id=sum_peer(phase, step), device_id_type=MESH
            )
            greeted += 1
    for neighbour in (above_row, below_row):
        pl.semaphore_signal(barrier, inc=1, device_id=(neighbour, group), device_id_type=MESH)
        greeted += 1

    loads = [
        pltpu.make_async_copy(source, target, local_sem.at[number])
        for number, (source, target) in enumerate(
            ((mask_hbm, mask), (prec_hbm, prec), (obs_hbm, obs), (edge_hbm, edge), (inv_hbm, inv), (tau_hbm, tau_ref))
        )
    ]
    for load in loads:
        load.start()

    for load in loads[:3]:
        load.wait()
    for date in range(dates_here):
        here = mask[date].astype(jnp.float32) * prec[date]
        weight_date[date] = here
        rhs_date[date] = here * obs[date]
    for date in range(dates_here):
        rhs[group * dates_here + date] = rhs_date[date, :, my_columns]
        weight[group * dates_here + date] = weight_date[date, :, my_columns]
    pl.semaphore_wait(barrier, greeted)

    def inward(field, source, target, step):
        peer = (group + step) % groups
        came_from = (group + groups - step) % groups
        block = source.at[:, :, pl.ds(pl.multiple_of(peer * width, width), width)]
        sent = pltpu.make_async_remote_copy(
            block, target.at[pl.ds(group * dates_here, dates_here)],
            send_sem.at[field, peer], recv_sem.at[field, group], (row, peer), MESH,
        )
        got = pltpu.make_async_remote_copy(
            block, target.at[pl.ds(came_from * dates_here, dates_here)],
            send_sem.at[field, peer], recv_sem.at[field, came_from], (row, peer), MESH,
        )
        return sent, got

    def outward(field, source, first, target, step):
        peer = (group + step) % groups
        came_from = (group + groups - step) % groups
        block = source.at[pl.ds(first + peer * dates_here, dates_here)]
        sent = pltpu.make_async_remote_copy(
            block, target.at[:, :, my_columns],
            send_sem.at[field, peer], recv_sem.at[field, group], (row, peer), MESH,
        )
        got = pltpu.make_async_remote_copy(
            block, target.at[:, :, pl.ds(pl.multiple_of(came_from * width, width), width)],
            send_sem.at[field, peer], recv_sem.at[field, came_from], (row, peer), MESH,
        )
        return sent, got

    half = groups // 2
    steps = sorted(range(1, groups), key=lambda step: (-min(step, groups - step), step))
    assert half >= 1
    rhs_copies = [inward(RHS, rhs_date, rhs, step) for step in steps]
    weight_copies = [inward(WEIGHT, weight_date, weight, step) for step in steps]
    for sent, _ in rhs_copies:
        sent.start()
    for sent, _ in weight_copies:
        sent.start()

    loads[3].wait()
    lane = lax.broadcasted_iota(jnp.int32, (height, LANES), 1)
    col = lax.broadcasted_iota(jnp.int32, (height, width), 1)
    line = lax.broadcasted_iota(jnp.int32, (height, width), 0)
    steps_across = 0.25 * (edge[0, :, my_columns].astype(jnp.float32) + 1.0)
    steps_down = 0.25 * (edge[1, :, my_columns].astype(jnp.float32) + 1.0)
    across[...] = jnp.where((col == width - 1) & (group == groups - 1), 0.0, steps_across)
    before = (left_group + 1) * width - LANES
    edge_before = edge[0, :, pl.ds(pl.multiple_of(before, LANES), LANES)].astype(jnp.float32)
    edge_before = pltpu.roll(0.25 * (edge_before + 1.0), 1, 1)
    edge_before = jnp.where(group == 0, 0.0, edge_before)

    def with_first(block, tile):
        first = jnp.where(lane == 0, tile, block[:, :LANES])
        if width == LANES:
            return first
        return jnp.concatenate([first, block[:, LANES:]], axis=1)

    def with_last(block, tile):
        last = jnp.where(lane == LANES - 1, tile, block[:, width - LANES :])
        if width == LANES:
            return last
        return jnp.concatenate([block[:, : width - LANES], last], axis=1)

    across_prev[...] = with_first(pltpu.roll(steps_across, 1, 1), edge_before)
    down_here = jnp.where((line == height - 1) & (row == rows - 1), 0.0, steps_down)
    downward[...] = down_here
    down_send[0, dates:, :] = jnp.broadcast_to(
        down_here[height - 1 :, :], (down_send.shape[1] - dates, width)
    )
    down_send[1, dates:, :] = jnp.zeros((down_send.shape[1] - dates, width), jnp.float32)
    rest = slice(dates_here, height)
    all_down = 0.25 * (edge[1, height - 1 :, :].astype(jnp.float32) + 1.0)
    for turn in range(2):
        date_down_send[turn, rest, :] = jnp.broadcast_to(all_down, (height - dates_here, columns))
        date_up_send[turn, rest, :] = jnp.zeros((height - dates_here, columns), jnp.float32)
    for field in (precond, mapped):
        field[0] = jnp.zeros((height, width), jnp.float32)
        field[dates + 1] = jnp.zeros((height, width), jnp.float32)

    def folded(block):
        total = block[:, :LANES]
        for start in range(LANES, width, LANES):
            total = total + block[:, start : start + LANES]
        return total

    def over_dates(step_of, init):
        def several(index, carry):
            for inner in range(UNROLL):
                carry = step_of(index * UNROLL + inner, carry)
            return carry

        return lax.fori_loop(0, dates // UNROLL, several, init)

    none = jnp.zeros((height, LANES), jnp.float32)

    def precondition(source, target, turn):
        def one(date, carry):
            total, to_right, to_left = carry
            out = inv[date, 0].astype(jnp.float32) * source[0]
            for other in range(1, dates):
                out = out + inv[date, other].astype(jnp.float32) * source[other]
            target[date + 1] = out
            down_send[turn, pl.ds(date, 1), :] = out[height - 1 :, :]
            up_send[turn, pl.ds(date, 1), :] = out[:1, :]
            to_right = jnp.where(
                lane == date, pltpu.roll(out[:, width - LANES :], date + 1, 1), to_right
            )
            to_left = jnp.where(lane == date, pltpu.roll(out[:, :LANES], date, 1), to_left)
            return total + folded(source[date] * out), to_right, to_left

        total, to_right, to_left = over_dates(one, (none, none, none))
        right_send[turn] = to_right
        left_send[turn] = to_left
        return total

    def halo(turn):
        pairs = (
            (down_send, from_above, (below_row, group)),
            (up_send, from_below, (above_row, group)),
            (right_send, from_left, (row, right_group)),
            (left_send, from_right, (row, left_group)),
        )
        return [
            pltpu.make_async_remote_copy(
                source.at[turn], target.at[turn],
                halo_send_sem.at[turn, number], halo_recv_sem.at[turn, number], device, MESH,
            )
            for number, (source, target, device) in enumerate(pairs)
        ]

    def operator(field, target, turn):
        def one(date, total):
            here = field[date + 1]
            above = jnp.where(
                line == 0, from_above[turn, pl.ds(date, 1), :], pltpu.roll(here, 1, 0)
            )
            below = jnp.where(
                line == height - 1,
                from_below[turn, pl.ds(date, 1), :],
                pltpu.roll(here, height - 1, 0),
            )
            left = with_first(
                pltpu.roll(here, 1, 1),
                pltpu.roll(from_left[turn], (LANES - date) % LANES, 1),
            )
            right = with_last(
                pltpu.roll(here, width - 1, 1),
                pltpu.roll(from_right[turn], LANES - 1 - date, 1),
            )
            tau_up = jnp.where(date < dates - 1, tau_ref[jnp.minimum(date, dates - 2)], 0.0)
            tau_down = jnp.where(date > 0, tau_ref[jnp.maximum(date - 1, 0)], 0.0)
            out = (MASS + weight[date]) * here
            out = out + across[...] * (here - right) + across_prev[...] * (here - left)
            out = out + downward[...] * (here - below) + downward_prev[...] * (here - above)
            out = out + tau_up * (here - field[date + 2])
            out = out + tau_down * (here - field[date])
            if target is not None:
                target[date] = out
            return total + folded(here * out)

        return over_dates(one, none)

    def bring_back(field, source, first, target, chosen=steps):
        copies = [outward(field, source, first, target, step) for step in chosen]
        for sent, _ in copies:
            sent.start()
        if chosen[-1] != steps[-1]:
            return copies
        for date in range(dates_here):
            target[date, :, my_columns] = source[first + group * dates_here + date]
        return copies

    loads[4].wait()
    loads[5].wait()
    for _, got in rhs_copies:
        got.wait_recv()
    sum_rz = precondition(rhs, precond, 0)
    first_halo = halo(0)
    for copy in first_halo:
        copy.start()
    early = len(steps) // 3
    precond_copies = bring_back(PRECOND, precond, 1, precond_date, steps[:early])
    for _, got in weight_copies:
        got.wait_recv()
    for copy in first_halo:
        copy.wait_recv()
    downward_prev[...] = jnp.where(
        line == 0,
        jnp.where(row == 0, 0.0, from_above[0, dates : dates + 1, :]),
        pltpu.roll(downward[...], 1, 0),
    )
    sum_d = operator(precond, image, 0)
    sum_e = precondition(image, mapped, 1)
    second_halo = halo(1)
    for copy in second_halo:
        copy.start()
    precond_copies += bring_back(PRECOND, precond, 1, precond_date, steps[early:])
    for copy in second_halo:
        copy.wait_recv()
    sum_f = operator(mapped, None, 1)

    def date_halo(turn, field, copies):
        for _, got in copies:
            got.wait_recv()
        for date in range(dates_here):
            date_down_send[turn, date : date + 1, :] = field[date, height - 1 :, :]
            date_up_send[turn, date : date + 1, :] = field[date, :1, :]
        pairs = (
            (date_down_send.at[turn], from_above_date, (below_row, group)),
            (date_up_send.at[turn], from_below_date, (above_row, group)),
            (field.at[dates_here - 1], from_before, (row, right_group)),
            (field.at[0], from_after, (row, left_group)),
        )
        started = [
            pltpu.make_async_remote_copy(
                source, target.at[turn],
                date_send_sem.at[turn, number], date_recv_sem.at[turn, number], device, MESH,
            )
            for number, (source, target, device) in enumerate(pairs)
        ]
        for copy in started:
            copy.start()
        return started

    tile_line = lax.broadcasted_iota(jnp.int32, (height, LANES), 0)
    tile = jnp.zeros((height, LANES), jnp.float32)
    for number, total in enumerate((sum_rz, sum_d, sum_e, sum_f)):
        tile = jnp.where(tile_line == number, jnp.sum(total, axis=0, keepdims=True), tile)
    sum_copies = []
    for phase, (size, mine) in enumerate(phases):
        part[phase] = tile
        parts[phase, mine] = tile
        received = []
        for step in range(1, size):
            came_from = (mine + size - step) % size
            sent = pltpu.make_async_remote_copy(
                part.at[phase], parts.at[phase, mine],
                sum_send_sem.at[phase, step], sum_recv_sem.at[phase, mine],
                sum_peer(phase, step), MESH,
            )
            sent.start()
            sum_copies.append(sent)
            received.append(
                pltpu.make_async_remote_copy(
                    part.at[phase], parts.at[phase, came_from],
                    sum_send_sem.at[phase, step], sum_recv_sem.at[phase, came_from],
                    sum_peer(phase, step), MESH,
                )
            )
        if phase == 0:
            mapped_copies = bring_back(MAPPED, mapped, 1, mapped_date)
            precond_halo = date_halo(0, precond_date, precond_copies)
        if phase == 2:
            mapped_halo = date_halo(1, mapped_date, mapped_copies)
        for got in received:
            got.wait_recv()
        tile = parts[phase, 0]
        for other in range(1, size):
            tile = tile + parts[phase, other]
    lines = jnp.sum(tile, axis=1, keepdims=True)
    rz, dd, ee, ff = (lines[number : number + 1] for number in range(4))
    alpha = rz / dd
    grown = alpha * ee / dd
    alpha_next = (alpha * alpha * ee - rz) / (alpha * alpha * (ff - ee * ee / dd))
    first = alpha + alpha_next * grown
    second = alpha_next * alpha
    first = jnp.broadcast_to(first, (height, width))
    second = jnp.broadcast_to(second, (height, width))

    def combined(at_precond, at_mapped):
        return first * at_precond - second * at_mapped

    spans = [slice(number * width, (number + 1) * width) for number in range(groups)]
    for date in range(dates_here):
        for span in spans:
            sol_ref[date, :, span] = combined(
                precond_date[date, :, span], mapped_date[date, :, span]
            )
    for copy in precond_halo[:2] + mapped_halo[:2]:
        copy.wait_recv()

    between = []
    for date in range(dates_here + 1):
        when = group * dates_here + date
        inside = (when > 0) & (when < dates)
        place = jnp.minimum(jnp.maximum(when - 1, 0), dates - 2)
        between.append(jnp.where(inside, tau_ref[place], 0.0))

    for number, span in enumerate(spans):
        tile_before = slice(max(span.start - LANES, 0), max(span.start, LANES))
        tile_after = slice(min(span.stop, columns - LANES), min(span.stop + LANES, columns))
        ahead = 0.25 * (edge[0, :, span].astype(jnp.float32) + 1.0)
        behind = 0.25 * (edge[0, :, tile_before].astype(jnp.float32) + 1.0)
        behind = with_first(pltpu.roll(ahead, 1, 1), pltpu.roll(behind, 1, 1))
        if number == 0:
            behind = jnp.where(col == 0, 0.0, behind)
        if number == groups - 1:
            ahead = jnp.where(col == width - 1, 0.0, ahead)
        under = 0.25 * (edge[1, :, span].astype(jnp.float32) + 1.0)
        under = jnp.where((line == height - 1) & (row == rows - 1), 0.0, under)
        over = jnp.where(
            line == 0,
            jnp.where(row == 0, 0.0, from_above_date[0, dates_here : dates_here + 1, span]),
            pltpu.roll(under, 1, 0),
        )
        for date in range(dates_here):
            here = sol_ref[date, :, span]
            this = slice(date, date + 1)
            above = combined(from_above_date[0, this, span], from_above_date[1, this, span])
            below = combined(from_below_date[0, this, span], from_below_date[1, this, span])
            above = jnp.where(line == 0, above, pltpu.roll(here, 1, 0))
            below = jnp.where(line == height - 1, below, pltpu.roll(here, height - 1, 0))
            left = with_first(
                pltpu.roll(here, 1, 1), pltpu.roll(sol_ref[date, :, tile_before], 1, 1)
            )
            right = with_last(
                pltpu.roll(here, width - 1, 1),
                pltpu.roll(sol_ref[date, :, tile_after], LANES - 1, 1),
            )
            out = (MASS + weight_date[date, :, span]) * here
            out = out + ahead * (here - right) + behind * (here - left)
            out = out + under * (here - below) + over * (here - above)
            if date > 0:
                out = out + between[date] * (here - sol_ref[date - 1, :, span])
            if date + 1 < dates_here:
                out = out + between[date + 1] * (here - sol_ref[date + 1, :, span])
            res_ref[date, :, span] = rhs_date[date, :, span] - out
    for copy in precond_halo[2:] + mapped_halo[2:]:
        copy.wait_recv()
    for span in spans:
        for date, weight_out, other in (
            (0, between[0], from_before),
            (dates_here - 1, between[dates_here], from_after),
        ):
            there = combined(other[0, :, span], other[1, :, span])
            res_ref[date, :, span] = res_ref[date, :, span] - weight_out * (
                sol_ref[date, :, span] - there
            )
    back = (precond_copies, mapped_copies)
    for copies in (rhs_copies, weight_copies) + back:
        for sent, _ in copies:
            sent.wait_send()
    for copy in first_halo + second_halo + precond_halo + mapped_halo + sum_copies:
        copy.wait_send()


def body(obs_mask, precision, observed, edge_class, temporal_weight, inverse):
    rows, groups = lax.axis_size("rows"), lax.axis_size("dates")
    low_size = 8 if rows >= 64 else 2
    dates, _, height, width = inverse.shape
    f32 = jnp.float32
    whole = observed.shape
    block = (dates, height, width)
    padded = (dates + 2, height, width)
    most = max(groups, low_size, rows // low_size)
    vmem = pltpu.VMEM
    dma = pltpu.SemaphoreType.DMA
    scratch = (
        [vmem(whole, jnp.int32), vmem(whole, f32), vmem(whole, f32)]
        + [vmem(edge_class.shape, jnp.int32), vmem(inverse.shape, jnp.bfloat16)]
        + [vmem(whole, f32)] * 4
        + [vmem(block, f32), vmem(block, f32), vmem(padded, f32), vmem(block, f32)]
        + [vmem(padded, f32)]
        + [vmem((2, height, whole[2]), f32)] * 6
        + [vmem((height, width), f32)] * 4
        + [vmem((2, dates + 8, width), f32), vmem((2, dates, width), f32)] * 2
        + [vmem((2, height, LANES), f32)] * 4
        + [vmem((3, height, LANES), f32), vmem((3, most, height, LANES), f32)]
        + [pltpu.SMEM((dates - 1,), f32), dma((6,)), dma((4, groups)), dma((4, groups))] + [dma((2, 4))] * 4
        + [dma((3, most)), dma((3, most))]
    )
    anywhere = pl.BlockSpec(memory_space=pltpu.HBM)
    in_hbm = [
        pltpu.with_memory_space_constraint(array, pltpu.HBM)
        for array in (obs_mask, precision, observed, edge_class, temporal_weight, inverse)
    ]
    return pl.pallas_call(
        functools.partial(kernel, rows, groups, low_size),
        out_shape=[jax.ShapeDtypeStruct(whole, f32)] * 2,
        in_specs=[anywhere] * 6,
        out_specs=[pl.BlockSpec(memory_space=pltpu.VMEM)] * 2,
        scratch_shapes=scratch,
        compiler_params=pltpu.CompilerParams(collective_id=0, has_side_effects=True, vmem_limit_bytes=VMEM_BYTES),
        name="cg",
    )(*in_hbm)


def solution(mesh):
    return jax.shard_map(
        body,
        mesh=mesh,
        in_specs=(
            P("dates", "rows", None),
            P("dates", "rows", None),
            P("dates", "rows", None),
            P(None, "rows", None),
            P(),
            P(None, None, "rows", "dates"),
        ),
        out_specs=(P("dates", "rows", None), P("dates", "rows", None)),
        check_vma=False,
    )
```
